512 devices in a mesh: kv: 64 (over x, z, core), tp: 8 (over y).
Axes of the slice: x: 4, y: 8, z: 8, core: 2. Of those that a mesh axis runs over, the one named last changes fastest.
Arguments:
- queries: bfloat16 [512, 7168], P('kv', 'tp'), may hold values from -30 to 30
- new_keys: bfloat16 [512, 7168], P('kv', 'tp'), may hold values from -6 to 6
- new_values: bfloat16 [512, 7168], P('kv', 'tp'), may hold values from -6 to 6
- keys: bfloat16 [24576, 7168], P('kv', 'tp'), may hold values from -8 to 8
- values: bfloat16 [24576, 7168], P('kv', 'tp'), may hold values from -6 to 6
- slot_request: int32 [24576], P('kv'), may hold values from 0 to 511, as said below
- slot_valid: int32 [24576], P('kv'), may hold values from 0 to 1, as said below
- out_weight: bfloat16 [7168, 7168], P('tp', 'kv'), may hold values from -0.0625 to 0.0625
- out_bias: bfloat16 [7168], P('kv'), may hold values from -3 to 3
- residual: bfloat16 [512, 7168], P('tp', 'kv'), may hold values from -6 to 6
Outputs:
- layer_out: bfloat16 [512, 7168], P('tp', 'kv')
The draws below stay inside these ranges and needn't reach their ends.
Inputs may be any that keep to these rules, and one draw needn't show every extreme that they name: `slot_request`: slots come in pages of 16 consecutive slots owned by one request; a request's pages are consecutive and may span several holders; every request owns at least one page and at most 514 pages, and one request owns exactly 514. `slot_valid`: only the last page of each request has empty slots, and that page holds at least one cached token in its first slot.
All inputs are finite; a program needn't handle non-finite values.
Results may differ from the reference program's by a relative error of at most 0.0033.
Values may be sent and summed in bfloat16 or wider, within the bound.
A program may use at most 64 MiB of HBM per device.

```python
import math
import jax
import jax.numpy as jnp
from jax import lax

D = 7168
HEADS = 56
HD = 128
PAGE = 16
REQS = 512
PAGES = 1536
SLOTS_DEV = 384
SLOTS = 24576
MAXPAGES = 514
N_KV = 64


def layout(key):
    base = jax.random.fold_in(key, 11)
    key_long, key_owner, key_order, key_fill = jax.random.split(base, 4)
    spare = PAGES - REQS - (MAXPAGES - 1)
    request_ids = jnp.arange(REQS, dtype=jnp.int32)
    long_request = jax.random.randint(key_long, (), 0, REQS, dtype=jnp.int32)
    owners = jax.random.randint(key_owner, (spare,), 0, REQS - 1, dtype=jnp.int32)
    owners = owners + (owners >= long_request).astype(jnp.int32)
    extra = jnp.sum((owners[:, None] == request_ids[None, :]).astype(jnp.int32), axis=0)
    counts = 1 + extra + (MAXPAGES - 1) * (request_ids == long_request).astype(jnp.int32)
    order = jax.random.permutation(key_order, REQS).astype(jnp.int32)
    ends = jnp.cumsum(counts[order]).astype(jnp.int32)
    page_ids = jnp.arange(PAGES, dtype=jnp.int32)
    position = jnp.sum((page_ids[:, None] >= ends[None, :]).astype(jnp.int32), axis=1)
    page_request = order[position]
    last_page = page_ids == ends[position] - 1
    fill = jax.random.randint(key_fill, (REQS,), 1, PAGE + 1, dtype=jnp.int32)
    slot_ids = jnp.arange(SLOTS, dtype=jnp.int32)
    slot_page = slot_ids // PAGE
    within = slot_ids % PAGE
    slot_owner = page_request[slot_page]
    empty = jnp.logical_and(last_page[slot_page], within >= fill[slot_owner])
    slot_live = jnp.where(empty, 0, 1).astype(jnp.int32)
    return (slot_owner.astype(jnp.int32), slot_live)


def draw_slot_request(key, part):
    slot_owner, slot_live = layout(key)
    return slot_owner


def draw_slot_valid(key, part):
    slot_owner, slot_live = layout(key)
    return slot_live


def draw_queries(key, part):
    noise_key = jax.random.fold_in(key, 31)
    noise = jnp.clip(jax.random.normal(noise_key, (REQS, D), jnp.float32), -6.0, 6.0)
    drawn = noise
    return jnp.clip(drawn, -30.0, 30.0).astype(jnp.bfloat16)


def draw_keys(key, part):
    noise_key = jax.random.fold_in(key, 51)
    noise = jnp.clip(jax.random.normal(noise_key, (SLOTS, D), jnp.float32), -6.0, 6.0)
    drawn = noise
    return jnp.clip(drawn, -8.0, 8.0).astype(jnp.bfloat16)


def level_of(stream_key, shape, cuts, low, largest):
    gain = 1.0
    for axis_at, parts in cuts:
        draws = jax.random.uniform(jax.random.fold_in(jax.random.fold_in(stream_key, 6), axis_at), (parts,), jnp.float32, low / len(cuts), largest / len(cuts))
        gain = gain * jnp.repeat(jnp.exp(draws), shape[axis_at] // parts).reshape((-1,) + (1,) * (len(shape) - 1 - axis_at))
    return gain


def normal_values(own_key, extent, width, bound, cuts=(), held_as=jnp.bfloat16):
    values = width * jax.random.normal(own_key, extent, jnp.float32)
    if cuts:
        values = values * level_of(own_key, extent, cuts, -0.22, 0.18)
    return jnp.clip(values, -bound, bound).astype(held_as)


def setup_inputs(seed: int = 0) -> dict:
    arg_keys = jax.random.split(jax.random.key(seed), 11)
    queries = draw_queries(jax.random.fold_in(arg_keys[10], 71), 0)
    new_keys = normal_values(arg_keys[1], (REQS, D), 1.0, 6.0, ((0, 64), (1, 8)))
    new_values = normal_values(arg_keys[2], (REQS, D), 1.0, 6.0, ((0, 64), (1, 8)))
    keys = draw_keys(jax.random.fold_in(arg_keys[10], 71), 0)
    values = normal_values(arg_keys[4], (SLOTS, D), 1.0, 6.0, ((0, 64), (1, 8)))
    slot_request = draw_slot_request(jax.random.fold_in(arg_keys[10], 71), 0)
    slot_valid = draw_slot_valid(jax.random.fold_in(arg_keys[10], 71), 0)
    out_weight = normal_values(arg_keys[7], (D, D), D ** -0.5, 0.0625, ((0, 8), (1, 64)))
    out_bias = normal_values(arg_keys[8], (D,), 0.5, 3.0, ((0, 64),))
    residual = normal_values(arg_keys[9], (REQS, D), 1.0, 6.0, ((0, 8), (1, 64)))
    return dict(queries=queries, new_keys=new_keys, new_values=new_values, keys=keys, values=values, slot_request=slot_request, slot_valid=slot_valid, out_weight=out_weight, out_bias=out_bias, residual=residual)


floor_score = -1e+30

def settle(x):
    return lax.optimization_barrier(x.astype(jnp.bfloat16)).astype(jnp.float32)

def reference(queries, new_keys, new_values, keys, values, slot_request, slot_valid, out_weight, out_bias, residual):
    score_scale = 1.0 / math.sqrt(HD)
    query_heads = queries.astype(jnp.float32).reshape(REQS, HEADS, HD)
    self_scores = lax.optimization_barrier(jnp.sum(query_heads * new_keys.astype(jnp.float32).reshape(REQS, HEADS, HD), axis=-1)) * score_scale
    key_blocks = keys.reshape(N_KV, SLOTS_DEV, D)
    value_blocks = values.reshape(N_KV, SLOTS_DEV, D)
    request_blocks = slot_request.reshape(N_KV, SLOTS_DEV).astype(jnp.int32)
    valid_blocks = slot_valid.reshape(N_KV, SLOTS_DEV)

    def block_scores(key_block, request_block, valid_block):
        picked = query_heads[request_block]
        scores = lax.optimization_barrier(jnp.sum(picked * key_block.astype(jnp.float32).reshape(SLOTS_DEV, HEADS, HD), axis=-1)) * score_scale
        return jnp.where((valid_block == 1)[:, None], scores, floor_score)

    def max_step(row_top, blocks):
        key_block, value_block, request_block, valid_block = blocks
        scores = block_scores(key_block, request_block, valid_block)
        return (row_top.at[request_block].max(scores), None)
    row_top, _ = lax.scan(max_step, self_scores, (key_blocks, value_blocks, request_blocks, valid_blocks))
    self_weight = settle(jnp.exp(self_scores - row_top))
    numer_start = self_weight[:, :, None] * new_values.astype(jnp.float32).reshape(REQS, HEADS, HD)

    def sum_step(carry, blocks):
        numer, denom = carry
        key_block, value_block, request_block, valid_block = blocks
        scores = block_scores(key_block, request_block, valid_block)
        weights = settle(jnp.where((valid_block == 1)[:, None], jnp.exp(scores - row_top[request_block]), 0.0))
        weighted = weights[:, :, None] * value_block.astype(jnp.float32).reshape(SLOTS_DEV, HEADS, HD)
        numer = numer + jax.ops.segment_sum(weighted, request_block, num_segments=REQS)
        denom = denom + jax.ops.segment_sum(weights, request_block, num_segments=REQS)
        return ((numer, denom), None)
    (numer, denom), _ = lax.scan(sum_step, (numer_start, self_weight), (key_blocks, value_blocks, request_blocks, valid_blocks))
    attended = (numer / denom[:, :, None]).reshape(REQS, D).astype(jnp.bfloat16)
    projected = jnp.dot(attended, out_weight, preferred_element_type=jnp.float32)
    total = residual.astype(jnp.float32) + projected + out_bias.astype(jnp.float32)[None, :]
    return total.astype(jnp.bfloat16)
```

```python
import math

import jax
import jax.numpy as jnp
from jax import lax
from jax.experimental import pallas as pl
from jax.experimental.pallas import tpu as pltpu
from jax.sharding import PartitionSpec as P

HD = 128
HEADS = 7
FEAT = HEADS * HD
WIDE = FEAT + 128
PAGE = 16
NX, NZ, NT, NB = 4, 8, 8, 8
ROWS = 8
FLOOR = -1e30
SCALE = 1.0 / math.sqrt(HD)
MESH = pl.DeviceIdType.MESH
F32, BF16 = jnp.float32, jnp.bfloat16

FAR_FIRST = (4, 3, 5, 2, 6, 1, 7)


def kv_of(x, z, c):
    return (x * NZ + z) * 2 + c


def split3(tile):
    lane = lax.broadcasted_iota(jnp.int32, tile.shape, 1)
    tile = jnp.where(lane < 8, tile, 0.0)
    high = tile.astype(BF16).astype(F32)
    middle = (tile - high).astype(BF16).astype(F32)
    low = tile - high - middle
    return high + pltpu.roll(middle, 8, 1) + pltpu.roll(low, 16, 1)


def join3(tile):
    axis = tile.ndim - 1
    return tile + pltpu.roll(tile, 128 - 8, axis) + pltpu.roll(tile, 128 - 16, axis)


def kernel(
    q_ref, nk_ref, nv_ref, sr_ref, sv_ref, k_hbm, v_hbm, w_hbm, out_ref,
    k_ref, v_ref, w_ref, wg, idc, qz, qs, qr, ob, cb, rb, sb, az, pc, cr, fs, fr,
    local, w_s, w_r, f_s, f_r, id_s, id_r, a1_s, a1_r, a2_s, a2_r, b1_s, b1_r, b2_s, b2_r,
    b3_s, b3_r, c1_s, c1_r, c2_s, c2_r, self_s, self_r,
):
    k = lax.axis_index("kv")
    t = lax.axis_index("tp")
    c = lax.rem(k, 2)
    xz = k // 2
    x = xz // NZ
    z = lax.rem(xz, NZ)
    b = x * 2 + c

    def to_kv(src, dst, send, recv, kv):
        return pltpu.make_async_remote_copy(
            src_ref=src, dst_ref=dst, send_sem=send, recv_sem=recv,
            device_id={"kv": kv}, device_id_type=MESH,
        )

    def to_tp(src, dst, send, recv, tp):
        return pltpu.make_async_remote_copy(
            src_ref=src, dst_ref=dst, send_sem=send, recv_sem=recv,
            device_id={"tp": tp}, device_id_type=MESH,
        )

    def z_at(d):
        return lax.rem(z + d, NZ)

    def b_at(e):
        return lax.rem(b + e, NB)

    def z_peer(d):
        return kv_of(x, z_at(d), c)

    def b_peer(e):
        other = b_at(e)
        return kv_of(other // 2, z, lax.rem(other, 2))

    def x_peer(d):
        return kv_of(lax.rem(x + d, NX), z, c)

    sibling = kv_of(x, z, 1 - c)
    owner = kv_of(lax.rem(z, 4), lax.rem(2 * x + z // 4 + 4, NZ), c)
    band = lax.rem(z + 4, NZ)
    home = kv_of(band // 2, lax.rem(band, 2) * 4 + x, c)

    loads = [
        pltpu.make_async_copy(w_hbm, w_ref, local.at[0]),
        pltpu.make_async_copy(k_hbm, k_ref, local.at[1]),
        pltpu.make_async_copy(v_hbm, v_ref, local.at[2]),
    ]
    for load in loads:
        load.start()

    barrier = pltpu.get_barrier_semaphore()
    for d in range(1, 8):
        pl.semaphore_signal(barrier, inc=1, device_id={"kv": z_peer(d)}, device_id_type=MESH)
        pl.semaphore_signal(barrier, inc=1, device_id={"kv": b_peer(d)}, device_id_type=MESH)
        pl.semaphore_signal(
            barrier, inc=1, device_id={"tp": lax.rem(t + d, NT)}, device_id_type=MESH
        )
    pl.semaphore_signal(barrier, inc=1, device_id={"kv": owner}, device_id_type=MESH)
    pl.semaphore_signal(barrier, inc=1, device_id={"kv": home}, device_id_type=MESH)

    slots = k_ref.shape[0]
    pages = slots // PAGE
    blocks = pages // ROWS
    lane_page = lax.broadcasted_iota(jnp.int32, (pages, slots), 1) // PAGE
    on_page = lane_page == lax.broadcasted_iota(jnp.int32, (pages, slots), 0)
    request_row = jnp.broadcast_to(sr_ref[...].astype(F32), (pages, slots))
    page_request = jnp.max(jnp.where(on_page, request_row, -1.0), axis=1, keepdims=True)
    live = jnp.where(on_page, jnp.broadcast_to(sv_ref[...], (pages, slots)), 0) == 1
    idc[b] = jnp.broadcast_to(page_request, (pages, 128))

    lane8 = lax.broadcasted_iota(jnp.int32, (ROWS, 128), 1)
    own = jnp.zeros((ROWS, 128), F32)
    for h in range(HEADS):
        head = slice(h * HD, (h + 1) * HD)
        product = q_ref[:, head].astype(F32) * nk_ref[:, head].astype(F32)
        own = jnp.where(lane8 == h, jnp.sum(product, axis=1, keepdims=True) * SCALE, own)
    sb[:, :FEAT] = nv_ref[...]
    sb[:, FEAT:] = split3(own).astype(BF16)

    qz[z] = q_ref[...]
    ob[:, blocks:] = jnp.zeros((NB, ob.shape[1] - blocks, ROWS, WIDE), BF16)

    pl.semaphore_wait(barrier, 23)

    sends = []

    def go(copy):
        copy.start()
        sends.append(copy)
        return copy

    a1 = [go(to_kv(q_ref, qz.at[z], a1_s.at[d], a1_r.at[d], z_peer(d))) for d in FAR_FIRST]
    ids = [go(to_kv(idc.at[b], idc.at[b], id_s.at[e], id_r.at[e], b_peer(e))) for e in FAR_FIRST]
    self_copy = go(to_kv(sb, rb.at[NZ], self_s, self_r, owner))
    loads[0].wait()
    columns = w_ref.shape[1]
    wg[b, :, :columns] = w_ref[...]
    wg[b, :, columns:] = jnp.zeros((w_ref.shape[0], 128 - columns), BF16)
    weight_x = [
        go(to_kv(wg.at[b], wg.at[b], w_s.at[d], w_r.at[d], x_peer(d))) for d in (2, 1, 3)
    ]
    weight_own = go(to_kv(wg.at[b], wg.at[b], w_s.at[0], w_r.at[0], sibling))

    for copy in ids + a1:
        copy.wait_recv()
    lane_q = lax.broadcasted_iota(jnp.int32, (NB * pages, NZ * ROWS), 1)
    lane_request = (x * 128 + (lane_q // ROWS) * 16 + c * ROWS + lax.rem(lane_q, ROWS)).astype(F32)
    wanted = idc[...].reshape(NB * pages, 128)[:, : NZ * ROWS]
    pick = jnp.where(wanted == lane_request, 1.0, 0.0).astype(BF16)
    line = qz[...].astype(F32).reshape(NZ * ROWS, FEAT).astype(BF16)
    picked = jnp.dot(pick, line, preferred_element_type=F32)
    qs[...] = picked.reshape(NB, blocks, ROWS, FEAT).astype(BF16)
    a2 = [go(to_kv(qs.at[b_at(e)], qr.at[b], a2_s.at[e], a2_r.at[e], b_peer(e))) for e in FAR_FIRST]
    qr[b] = qs[b]
    loads[1].wait()
    loads[2].wait()
    for copy in a2:
        copy.wait_recv()

    lane24 = lax.broadcasted_iota(jnp.int32, (pages, 128), 1)
    tops = jnp.zeros((pages, 128), F32)
    for h in range(HEADS):
        head = slice(h * HD, (h + 1) * HD)
        query = jnp.sum(qr[:, :, :, head].astype(F32), axis=0).reshape(pages, HD).astype(BF16)
        score = SCALE * lax.dot_general(
            query, k_ref[:, head], (((1,), (1,)), ((), ())), preferred_element_type=F32
        )
        score = jnp.where(live, score, FLOOR)
        top = jnp.max(score, axis=1, keepdims=True)
        weight = jnp.where(live, jnp.exp(score - top), 0.0).astype(BF16)
        total = jnp.sum(weight.astype(F32), axis=1, keepdims=True)
        part = jnp.dot(weight, v_ref[:, head], preferred_element_type=F32) / total
        ob[b, :blocks, :, head] = part.reshape(blocks, ROWS, HD).astype(BF16)
        tops = jnp.where(lane24 == h, top + jnp.log(total), tops)
    request_high = jnp.floor(page_request * 0.125)
    stats = split3(tops)
    stats = jnp.where(lane24 == 24, request_high + 1.0, stats)
    stats = jnp.where(lane24 == 25, page_request - 8.0 * request_high, stats)
    ob[b, :blocks, :, FEAT:] = stats.reshape(blocks, ROWS, 128).astype(BF16)
    mine = ob.at[b, pl.ds(0, blocks)]
    b1 = [go(to_kv(mine, mine, b1_s.at[e], b1_r.at[e], b_peer(e))) for e in FAR_FIRST]
    for copy in b1:
        copy.wait_recv()

    depth = NB * ob.shape[1] * ROWS
    count = NZ * ROWS
    turned = ob[:, :, :, FEAT:].astype(F32).reshape(depth, 128).T
    row_top = turned[0:8] + turned[8:16] + turned[16:24]
    row_request = turned[24:25] * 8.0 + turned[25:26]
    row_q = lax.broadcasted_iota(jnp.int32, (count, depth), 0)
    my_request = (
        lax.rem(row_q // ROWS + 4, NZ) * 64 + b * ROWS + lax.rem(row_q, ROWS) + 8
    ).astype(F32)
    match = jnp.broadcast_to(row_request, (count, depth)) == my_request
    lane64 = lax.broadcasted_iota(jnp.int32, (count, 128), 1)
    tops = jnp.full((count, 128), FLOOR, F32)
    for h in range(HEADS):
        head = slice(h * HD, (h + 1) * HD)
        level = jnp.where(match, jnp.broadcast_to(row_top[h : h + 1], (count, depth)), FLOOR)
        top = jnp.max(level, axis=1, keepdims=True)
        weight = jnp.where(match, jnp.exp(level - top), 0.0).astype(BF16)
        total = jnp.sum(weight.astype(F32), axis=1, keepdims=True)
        rows = ob[:, :, :, head].astype(F32).reshape(depth, HD).astype(BF16)
        some = total > 0.0
        safe = jnp.where(some, total, 1.0)
        part = jnp.dot(weight, rows, preferred_element_type=F32) / safe
        cb[:, :, head] = part.reshape(NZ, ROWS, HD).astype(BF16)
        tops = jnp.where(lane64 == h, jnp.where(some, top + jnp.log(safe), FLOOR), tops)
    cb[:, :, FEAT:] = split3(tops).reshape(NZ, ROWS, 128).astype(BF16)
    b2 = [go(to_kv(cb.at[z_at(d)], rb.at[z], b2_s.at[d], b2_r.at[d], z_peer(d))) for d in FAR_FIRST]
    rb[z] = cb[z]

    weight_on = []
    for copy, d in zip(weight_x, (2, 1, 3)):
        copy.wait_recv()
        block = wg.at[lax.rem(x + NX - d, NX) * 2 + c]
        weight_on.append(go(to_kv(block, block, f_s.at[d], f_r.at[d], sibling)))

    for copy in b2:
        copy.wait_recv()
    self_copy.wait_recv()

    level = join3(rb[:, :, FEAT:].astype(F32))
    share = jnp.exp(level - jnp.max(level, axis=0, keepdims=True))
    share = share / jnp.sum(share, axis=0, keepdims=True)
    for h in range(HEADS):
        head = slice(h * HD, (h + 1) * HD)
        part = jnp.sum(share[:, :, h : h + 1] * rb[:, :, head].astype(F32), axis=0)
        az[z, :, head] = part.astype(BF16)
    b3 = [go(to_kv(az.at[z], az.at[z], b3_s.at[d], b3_r.at[d], z_peer(d))) for d in FAR_FIRST]
    weight_own.wait_recv()
    for copy in weight_on + b3:
        copy.wait_recv()

    attended = az[...].astype(F32).reshape(count, FEAT).astype(BF16)
    for block in range(NB):
        product = jnp.dot(attended, wg[block], preferred_element_type=F32)
        pc[:, :, block * 128 : (block + 1) * 128] = product.reshape(NZ, ROWS, 128).astype(BF16)

    def band_at(d):
        return lax.rem(t + d + 4, NT)

    c1 = [
        go(to_tp(pc.at[band_at(d)], cr.at[t], c1_s.at[d], c1_r.at[d], lax.rem(t + d, NT)))
        for d in FAR_FIRST
    ]
    cr[t] = pc[band_at(0)]
    for copy in c1:
        copy.wait_recv()
    summed = jnp.sum(cr[...].astype(F32), axis=0)
    for block in range(NB):
        fs[block] = summed[:, block * 128 : (block + 1) * 128]
    c2 = [go(to_kv(fs.at[b_at(e)], fr.at[b], c2_s.at[e], c2_r.at[e], b_peer(e))) for e in FAR_FIRST]
    fr[b] = fs[b]
    for copy in c2:
        copy.wait_recv()
    out_ref[...] = fr[...].reshape(NB * ROWS, 128)
    for copy in sends:
        copy.wait_send()


def on_device(
    queries,
    new_keys,
    new_values,
    keys,
    values,
    slot_request,
    slot_valid,
    out_weight,
    out_bias,
    residual,
):
    slots = keys.shape[0]
    depth, columns = out_weight.shape
    pages = slots // PAGE
    blocks = pages // ROWS
    padded = 4
    vmem = pl.BlockSpec(memory_space=pltpu.VMEM)
    hbm = pl.BlockSpec(memory_space=pl.ANY)
    dma = pltpu.SemaphoreType.DMA
    pairs = [dma((NB,))] * 2
    projected = pl.pallas_call(
        kernel,
        out_shape=jax.ShapeDtypeStruct((NB * ROWS, 128), F32),
        in_specs=[vmem] * 5 + [hbm] * 3,
        out_specs=vmem,
        scratch_shapes=[
            pltpu.VMEM((slots, FEAT), BF16),
            pltpu.VMEM((slots, FEAT), BF16),
            pltpu.VMEM((depth, columns), BF16),
            pltpu.VMEM((NB, depth, 128), BF16),
            pltpu.VMEM((NB, pages, 128), F32),
            pltpu.VMEM((NZ, ROWS, FEAT), BF16),
            pltpu.VMEM((NB, blocks, ROWS, FEAT), BF16),
            pltpu.VMEM((NB, blocks, ROWS, FEAT), BF16),
            pltpu.VMEM((NB, padded, ROWS, WIDE), BF16),
            pltpu.VMEM((NZ, ROWS, WIDE), BF16),
            pltpu.VMEM((NZ + 1, ROWS, WIDE), BF16),
            pltpu.VMEM((ROWS, WIDE), BF16),
            pltpu.VMEM((NZ, ROWS, FEAT), BF16),
            pltpu.VMEM((NZ, ROWS, NB * 128), BF16),
            pltpu.VMEM((NT, ROWS, NB * 128), BF16),
            pltpu.VMEM((NB, ROWS, 128), F32),
            pltpu.VMEM((NB, ROWS, 128), F32),
            dma((3,)),
            dma((NX,)), dma((NX,)), dma((NX,)), dma((NX,)),
        ]
        + pairs * 8
        + [dma, dma],
        compiler_params=pltpu.CompilerParams(
            collective_id=0, has_side_effects=True, vmem_limit_bytes=40 << 20
        ),
        name="paged_decode",
    )(
        queries, new_keys, new_values, slot_request.reshape(1, slots),
        slot_valid.reshape(1, slots), keys, values, out_weight,
    )
    total = (
        residual.astype(F32) + projected[:, :columns] + out_bias.astype(F32)[None, :]
    )
    return total.astype(BF16)


def solution(mesh):
    placed = (
        P("kv", "tp"),
        P("kv", "tp"),
        P("kv", "tp"),
        P("kv", "tp"),
        P("kv", "tp"),
        P("kv"),
        P("kv"),
        P("tp", "kv"),
        P("kv"),
        P("tp", "kv"),
    )
    return jax.shard_map(
        on_device, mesh=mesh, in_specs=placed, out_specs=P("tp", "kv"), check_vma=False
    )
```

```python
import math

import jax
import jax.numpy as jnp
from jax import lax
from jax.experimental import pallas as pl
from jax.experimental.pallas import tpu as pltpu
from jax.sharding import PartitionSpec as P

HD = 128
HEADS = 7
FEAT = HEADS * HD
WIDE = FEAT + 128
PAGE = 16
NX, NZ, NT, NB = 4, 8, 8, 8
ROWS = 8
FLOOR = -1e30
SCALE = 1.0 / math.sqrt(HD)
MESH = pl.DeviceIdType.MESH
F32, BF16 = jnp.float32, jnp.bfloat16

FAR_FIRST = (4, 3, 5, 2, 6, 1, 7)

EARLY = 2


def kv_of(x, z, c):
    return (x * NZ + z) * 2 + c


def split3(tile):
    lane = lax.broadcasted_iota(jnp.int32, tile.shape, 1)
    tile = jnp.where(lane < 8, tile, 0.0)
    high = tile.astype(BF16).astype(F32)
    middle = (tile - high).astype(BF16).astype(F32)
    low = tile - high - middle
    return high + pltpu.roll(middle, 8, 1) + pltpu.roll(low, 16, 1)


def join3(tile):
    axis = tile.ndim - 1
    return tile + pltpu.roll(tile, 128 - 8, axis) + pltpu.roll(tile, 128 - 16, axis)


def kernel(
    q_hbm, nk_hbm, nv_hbm, sr_hbm, sv_hbm, k_hbm, v_hbm, w_hbm, out_ref,
    nk_ref, nv_ref, sr_ref, sv_ref, k_ref, v_ref, wg, idc, qz, qs, qr, ob, cb, rb, sb, az, pc, fr,
    local, w_s, w_r, f_s, f_r, id_s, id_r, a1_s, a1_r, a2_s, a2_r, b1_s, b1_r, b2_s, b2_r,
    b3_s, b3_r, c1_s, c1_r, self_s, self_r,
):
    k = lax.axis_index("kv")
    t = lax.axis_index("tp")
    c = lax.rem(k, 2)
    xz = k // 2
    x = xz // NZ
    z = lax.rem(xz, NZ)
    b = x * 2 + c

    def to_kv(src, dst, send, recv, kv):
        return pltpu.make_async_remote_copy(
            src_ref=src, dst_ref=dst, send_sem=send, recv_sem=recv,
            device_id={"kv": kv}, device_id_type=MESH,
        )

    def to_tp(src, dst, send, recv, tp):
        return pltpu.make_async_remote_copy(
            src_ref=src, dst_ref=dst, send_sem=send, recv_sem=recv,
            device_id={"tp": tp}, device_id_type=MESH,
        )

    def z_at(d):
        return lax.rem(z + d, NZ)

    def b_at(e):
        return lax.rem(b + e, NB)

    def z_peer(d):
        return kv_of(x, z_at(d), c)

    def b_peer(e):
        other = b_at(e)
        return kv_of(other // 2, z, lax.rem(other, 2))

    def x_peer(d):
        return kv_of(lax.rem(x + d, NX), z, c)

    sibling = kv_of(x, z, 1 - c)
    owner = kv_of(lax.rem(z, 4), lax.rem(2 * x + z // 4 + 4, NZ), c)

    barrier = pltpu.get_barrier_semaphore()
    for d in range(1, 8):
        pl.semaphore_signal(barrier, inc=1, device_id={"kv": z_peer(d)}, device_id_type=MESH)
        pl.semaphore_signal(barrier, inc=1, device_id={"kv": b_peer(d)}, device_id_type=MESH)
        pl.semaphore_signal(
            barrier, inc=1, device_id={"tp": lax.rem(t + d, NT)}, device_id_type=MESH
        )

    small = [
        pltpu.make_async_copy(sr_hbm, sr_ref, local.at[1]),
        pltpu.make_async_copy(sv_hbm, sv_ref, local.at[2]),
        pltpu.make_async_copy(q_hbm, qz.at[z], local.at[0]),
        pltpu.make_async_copy(nk_hbm, nk_ref, local.at[3]),
        pltpu.make_async_copy(nv_hbm, nv_ref, local.at[4]),
    ]
    large = [
        pltpu.make_async_copy(w_hbm, wg.at[b], local.at[5]),
        pltpu.make_async_copy(k_hbm, k_ref, local.at[6]),
        pltpu.make_async_copy(v_hbm, v_ref, local.at[7]),
    ]
    for load in small + large:
        load.start()

    sends = []

    def go(copy):
        copy.start()
        sends.append(copy)
        return copy

    def arrive(*copies):
        for copy in copies:
            copy.wait_recv()

    slots = k_ref.shape[0]
    pages = slots // PAGE
    blocks = pages // ROWS
    lane_page = lax.broadcasted_iota(jnp.int32, (pages, slots), 1) // PAGE
    on_page = lane_page == lax.broadcasted_iota(jnp.int32, (pages, slots), 0)
    small[0].wait()
    request_row = jnp.broadcast_to(sr_ref[...].reshape(1, slots).astype(F32), (pages, slots))
    page_request = jnp.max(jnp.where(on_page, request_row, -1.0), axis=1, keepdims=True)
    idc[b] = jnp.broadcast_to(page_request, (pages, 128))
    pl.semaphore_wait(barrier, 21)

    a1 = [go(to_kv(q_hbm, qz.at[z], a1_s.at[d], a1_r.at[d], z_peer(d))) for d in FAR_FIRST]
    ids = [go(to_kv(idc.at[b], idc.at[b], id_s.at[e], id_r.at[e], b_peer(e))) for e in FAR_FIRST]

    def weights_x(first, last):
        part = pl.ds(first, last - first)
        sem = 0 if first == 0 else NX
        return [
            go(to_kv(w_hbm.at[part], wg.at[b, part], w_s.at[sem + d], w_r.at[sem + d], x_peer(d)))
            for d in (2, 1, 3)
        ]

    def weights_on(copies, first, last):
        part = pl.ds(first, last - first)
        sem = 0 if first == 0 else NX
        done = []
        for copy, d in zip(copies, (2, 1, 3)):
            arrive(copy)
            block = wg.at[lax.rem(x + NX - d, NX) * 2 + c, part]
            done.append(go(to_kv(block, block, f_s.at[sem + d], f_r.at[sem + d], sibling)))
        return done

    chunks = wg.shape[1]
    early = weights_x(0, EARLY)
    weight_own = go(to_kv(w_hbm, wg.at[b], w_s.at[0], w_r.at[0], sibling))

    for load in small[1:]:
        load.wait()
    live_row = jnp.broadcast_to(sv_ref[...].reshape(1, slots), (pages, slots))
    live = jnp.where(on_page, live_row, 0) == 1
    lane8 = lax.broadcasted_iota(jnp.int32, (ROWS, 128), 1)
    own = jnp.zeros((ROWS, 128), F32)
    for h in range(HEADS):
        head = slice(h * HD, (h + 1) * HD)
        product = qz[z, :, head].astype(F32) * nk_ref[:, head].astype(F32)
        own = jnp.where(lane8 == h, jnp.sum(product, axis=1, keepdims=True) * SCALE, own)
    sb[:, :FEAT] = nv_ref[...]
    sb[:, FEAT:] = split3(own).astype(BF16)
    ob[:, blocks:] = jnp.zeros((NB, ob.shape[1] - blocks, ROWS, WIDE), BF16)

    arrive(*ids, *a1)
    lane_q = lax.broadcasted_iota(jnp.int32, (NB * pages, NZ * ROWS), 1)
    lane_request = (x * 128 + (lane_q // ROWS) * 16 + c * ROWS + lax.rem(lane_q, ROWS)).astype(F32)
    wanted = idc[...].reshape(NB * pages, 128)[:, : NZ * ROWS]
    pick = jnp.where(wanted == lane_request, 1.0, 0.0).astype(BF16)
    line = qz[...].astype(F32).reshape(NZ * ROWS, FEAT).astype(BF16)
    picked = jnp.dot(pick, line, preferred_element_type=F32)
    qs[...] = picked.reshape(NB, blocks, ROWS, FEAT).astype(BF16)
    a2 = [go(to_kv(qs.at[b_at(e)], qr.at[b], a2_s.at[e], a2_r.at[e], b_peer(e))) for e in FAR_FIRST]
    qr[b] = qs[b]
    large[1].wait()
    large[2].wait()
    arrive(*a2)
    self_copy = go(to_kv(sb, rb.at[NZ], self_s, self_r, owner))
    early_on = weights_on(early, 0, EARLY)

    lane24 = lax.broadcasted_iota(jnp.int32, (pages, 128), 1)
    tops = jnp.zeros((pages, 128), F32)
    for h in range(HEADS):
        head = slice(h * HD, (h + 1) * HD)
        query = jnp.sum(qr[:, :, :, head].astype(F32), axis=0).reshape(pages, HD).astype(BF16)
        score = SCALE * lax.dot_general(
            query, k_ref[:, head], (((1,), (1,)), ((), ())), preferred_element_type=F32
        )
        score = jnp.where(live, score, FLOOR)
        top = jnp.max(score, axis=1, keepdims=True)
        weight = jnp.where(live, jnp.exp(score - top), 0.0).astype(BF16)
        total = jnp.sum(weight.astype(F32), axis=1, keepdims=True)
        part = jnp.dot(weight, v_ref[:, head], preferred_element_type=F32) / total
        ob[b, :blocks, :, head] = part.reshape(blocks, ROWS, HD).astype(BF16)
        tops = jnp.where(lane24 == h, top + jnp.log(total), tops)
    request_high = jnp.floor(page_request * 0.125)
    stats = split3(tops)
    stats = jnp.where(lane24 == 24, request_high + 1.0, stats)
    stats = jnp.where(lane24 == 25, page_request - 8.0 * request_high, stats)
    ob[b, :blocks, :, FEAT:] = stats.reshape(blocks, ROWS, 128).astype(BF16)
    mine = ob.at[b, pl.ds(0, blocks)]
    b1 = [go(to_kv(mine, mine, b1_s.at[e], b1_r.at[e], b_peer(e))) for e in FAR_FIRST]
    arrive(*b1)
    late = weights_x(EARLY, chunks)

    depth = NB * ob.shape[1] * ROWS
    count = NZ * ROWS
    turned = ob[:, :, :, FEAT:].astype(F32).reshape(depth, 128).T
    row_top = turned[0:8] + turned[8:16] + turned[16:24]
    row_request = turned[24:25] * 8.0 + turned[25:26]
    row_q = lax.broadcasted_iota(jnp.int32, (count, depth), 0)
    my_request = (
        lax.rem(row_q // ROWS + 4, NZ) * 64 + b * ROWS + lax.rem(row_q, ROWS) + 8
    ).astype(F32)
    match = jnp.broadcast_to(row_request, (count, depth)) == my_request
    lane64 = lax.broadcasted_iota(jnp.int32, (count, 128), 1)
    tops = jnp.full((count, 128), FLOOR, F32)
    for h in range(HEADS):
        head = slice(h * HD, (h + 1) * HD)
        level = jnp.where(match, jnp.broadcast_to(row_top[h : h + 1], (count, depth)), FLOOR)
        top = jnp.max(level, axis=1, keepdims=True)
        weight = jnp.where(match, jnp.exp(level - top), 0.0).astype(BF16)
        total = jnp.sum(weight.astype(F32), axis=1, keepdims=True)
        rows = ob[:, :, :, head].astype(F32).reshape(depth, HD).astype(BF16)
        some = total > 0.0
        safe = jnp.where(some, total, 1.0)
        part = jnp.dot(weight, rows, preferred_element_type=F32) / safe
        cb[:, :, head] = part.reshape(NZ, ROWS, HD).astype(BF16)
        tops = jnp.where(lane64 == h, jnp.where(some, top + jnp.log(safe), FLOOR), tops)
    cb[:, :, FEAT:] = split3(tops).reshape(NZ, ROWS, 128).astype(BF16)
    b2 = [go(to_kv(cb.at[z_at(d)], rb.at[z], b2_s.at[d], b2_r.at[d], z_peer(d))) for d in FAR_FIRST]
    rb[z] = cb[z]

    arrive(*b2, self_copy)

    level = join3(rb[:, :, FEAT:].astype(F32))
    share = jnp.exp(level - jnp.max(level, axis=0, keepdims=True))
    share = share / jnp.sum(share, axis=0, keepdims=True)
    for h in range(HEADS):
        head = slice(h * HD, (h + 1) * HD)
        part = jnp.sum(share[:, :, h : h + 1] * rb[:, :, head].astype(F32), axis=0)
        az[z, :, head] = part.astype(BF16)
    b3 = [go(to_kv(az.at[z], az.at[z], b3_s.at[d], b3_r.at[d], z_peer(d))) for d in FAR_FIRST]
    late_on = weights_on(late, EARLY, chunks)
    arrive(*b3)
    arrive(weight_own, *early_on, *late_on)
    large[0].wait()

    attended = az[...].astype(F32).reshape(count, FEAT).astype(BF16)
    columns = chunks * 16
    c1 = []
    for e in FAR_FIRST + (0,):
        product = lax.dot_general(
            attended, wg[b_at(e)].reshape(columns, FEAT), (((1,), (1,)), ((), ())),
            preferred_element_type=F32,
        )
        pc[e, :, :, :columns] = product.reshape(NZ, ROWS, columns).astype(BF16)
        for d in FAR_FIRST + (0,):
            rows = lax.rem(t + d + 4, NT)
            if d == 0 and e == 0:
                fr[t * NB + b] = pc[e, rows]
                continue
            sem = d * NB + e
            c1.append(
                go(
                    pltpu.make_async_remote_copy(
                        src_ref=pc.at[e, rows], dst_ref=fr.at[t * NB + b],
                        send_sem=c1_s.at[sem], recv_sem=c1_r.at[sem],
                        device_id={"kv": b_peer(e), "tp": lax.rem(t + d, NT)},
                        device_id_type=MESH,
                    )
                )
            )
    arrive(*c1)
    out_ref[...] = jnp.sum(fr[...].astype(F32).reshape(NT, NB * ROWS, 128), axis=0)
    for copy in sends:
        copy.wait_send()


def on_device(
    queries,
    new_keys,
    new_values,
    keys,
    values,
    slot_request,
    slot_valid,
    out_weight,
    out_bias,
    residual,
):
    slots = keys.shape[0]
    columns = out_weight.shape[1]
    pages = slots // PAGE
    blocks = pages // ROWS
    padded = 4
    vmem = pl.BlockSpec(memory_space=pltpu.VMEM)
    hbm = pl.BlockSpec(memory_space=pltpu.HBM)
    dma = pltpu.SemaphoreType.DMA
    pairs = [dma((NB,))] * 2
    projected = pl.pallas_call(
        kernel,
        out_shape=jax.ShapeDtypeStruct((NB * ROWS, 128), F32),
        in_specs=[hbm] * 8,
        out_specs=vmem,
        scratch_shapes=[
            pltpu.VMEM((ROWS, FEAT), BF16),
            pltpu.VMEM((ROWS, FEAT), BF16),
            pltpu.VMEM((slots,), jnp.int32),
            pltpu.VMEM((slots,), jnp.int32),
            pltpu.VMEM((slots, FEAT), BF16),
            pltpu.VMEM((slots, FEAT), BF16),
            pltpu.VMEM((NB, columns // 16, 16, FEAT), BF16),
            pltpu.VMEM((NB, pages, 128), F32),
            pltpu.VMEM((NZ, ROWS, FEAT), BF16),
            pltpu.VMEM((NB, blocks, ROWS, FEAT), BF16),
            pltpu.VMEM((NB, blocks, ROWS, FEAT), BF16),
            pltpu.VMEM((NB, padded, ROWS, WIDE), BF16),
            pltpu.VMEM((NZ, ROWS, WIDE), BF16),
            pltpu.VMEM((NZ + 1, ROWS, WIDE), BF16),
            pltpu.VMEM((ROWS, WIDE), BF16),
            pltpu.VMEM((NZ, ROWS, FEAT), BF16),
            pltpu.VMEM((NB, NZ, ROWS, 128), BF16),
            pltpu.VMEM((NT * NB, ROWS, 128), BF16),
            dma((8,)),
            dma((2 * NX,)), dma((2 * NX,)), dma((2 * NX,)), dma((2 * NX,)),
        ]
        + pairs * 6
        + [dma((NT * NB,)), dma((NT * NB,)), dma, dma],
        compiler_params=pltpu.CompilerParams(
            collective_id=0, has_side_effects=True, vmem_limit_bytes=63 << 20
        ),
        name="paged_decode",
    )(
        queries, new_keys, new_values, slot_request, slot_valid, keys, values,
        out_weight.T.reshape(columns // 16, 16, FEAT),
    )
    total = (
        residual.astype(F32) + projected[:, :columns] + out_bias.astype(F32)[None, :]
    )
    return total.astype(BF16)


def solution(mesh):
    placed = (
        P("kv", "tp"),
        P("kv", "tp"),
        P("kv", "tp"),
        P("kv", "tp"),
        P("kv", "tp"),
        P("kv"),
        P("kv"),
        P("tp", "kv"),
        P("kv"),
        P("tp", "kv"),
    )
    return jax.shard_map(
        on_device, mesh=mesh, in_specs=placed, out_specs=P("tp", "kv"), check_vma=False
    )
```

```python
import math

import jax
import jax.numpy as jnp
from jax import lax
from jax.experimental import pallas as pl
from jax.experimental.pallas import tpu as pltpu
from jax.sharding import PartitionSpec as P

HD = 128
HEADS = 7
FEAT = HEADS * HD
PAGE = 16
NX, NZ, NT, NB = 4, 8, 8, 8
ROWS = 8
FLOOR = -1e30
SCALE = 1.0 / math.sqrt(HD)
MESH = pl.DeviceIdType.MESH
F32, BF16 = jnp.float32, jnp.bfloat16

GROUPS = ((0, 4), (4, 3))

FAR_FIRST = (4, 3, 5, 2, 6, 1, 7)

EARLY = 3

GRANT = 63 << 20


def kv_of(x, z, c):
    return (x * NZ + z) * 2 + c


def head_at(h):
    return slice(h * HD, (h + 1) * HD)


def split3(tile):
    lane = lax.broadcasted_iota(jnp.int32, tile.shape, 1)
    tile = jnp.where(lane < 8, tile, 0.0)
    high = tile.astype(BF16).astype(F32)
    middle = (tile - high).astype(BF16).astype(F32)
    low = tile - high - middle
    return high + pltpu.roll(middle, 8, 1) + pltpu.roll(low, 16, 1)


def join3(tile):
    axis = tile.ndim - 1
    return tile + pltpu.roll(tile, 128 - 8, axis) + pltpu.roll(tile, 128 - 16, axis)


def kernel(
    q_hbm, nk_hbm, nv_hbm, sr_hbm, sv_hbm, k_hbm, v_hbm, w_hbm, out_ref,
    nk_ref, nv_ref, sr_ref, sv_ref, k_ref, v_ref, wg, idc, qz, qs, qr, ob, cb, rb, sb, az,
    acc, pc, fr, local, w_s, w_r, f_s, f_r, id_s, id_r, a1_s, a1_r, a2_s, a2_r, b1_s, b1_r,
    b2_s, b2_r, b3_s, b3_r, self_s, self_r, c_s, c_r,
):
    k = lax.axis_index("kv")
    t = lax.axis_index("tp")
    c = lax.rem(k, 2)
    xz = k // 2
    x = xz // NZ
    z = lax.rem(xz, NZ)
    b = x * 2 + c

    def to_kv(src, dst, send, recv, kv):
        return pltpu.make_async_remote_copy(
            src_ref=src, dst_ref=dst, send_sem=send, recv_sem=recv,
            device_id={"kv": kv}, device_id_type=MESH,
        )

    def z_at(d):
        return lax.rem(z + d, NZ)

    def b_at(e):
        return lax.rem(b + e, NB)

    def z_peer(d):
        return kv_of(x, z_at(d), c)

    def b_peer(e):
        other = b_at(e)
        return kv_of(other // 2, z, lax.rem(other, 2))

    def x_peer(d):
        return kv_of(lax.rem(x + d, NX), z, c)

    sibling = kv_of(x, z, 1 - c)
    owner = kv_of(lax.rem(z, 4), lax.rem(2 * x + z // 4 + 4, NZ), c)

    barrier = pltpu.get_barrier_semaphore()
    for d in range(1, 8):
        pl.semaphore_signal(barrier, inc=1, device_id={"kv": z_peer(d)}, device_id_type=MESH)
    for d in range(1, 8):
        pl.semaphore_signal(barrier, inc=1, device_id={"kv": b_peer(d)}, device_id_type=MESH)
    for d in range(1, 8):
        pl.semaphore_signal(
            barrier, inc=1, device_id={"tp": lax.rem(t + d, NT)}, device_id_type=MESH
        )

    def feats(g):
        first, heads = GROUPS[g]
        return pl.ds(first * HD, heads * HD)

    groups = range(len(GROUPS))
    small = [
        pltpu.make_async_copy(sr_hbm, sr_ref, local.at[0]),
        pltpu.make_async_copy(sv_hbm, sv_ref, local.at[1]),
        pltpu.make_async_copy(nk_hbm, nk_ref, local.at[2]),
        pltpu.make_async_copy(nv_hbm, nv_ref, local.at[3]),
    ] + [
        pltpu.make_async_copy(q_hbm.at[:, feats(g)], qz[g].at[z], local.at[4 + g]) for g in groups
    ]
    large = [
        pltpu.make_async_copy(w_hbm, wg.at[b], local.at[6]),
        pltpu.make_async_copy(k_hbm, k_ref, local.at[7]),
        pltpu.make_async_copy(v_hbm, v_ref, local.at[8]),
    ]
    for load in small:
        load.start()

    sends = []

    def go(copy):
        copy.start()
        sends.append(copy)
        return copy

    def arrive(*copies):
        for copy in copies:
            copy.wait_recv()

    pl.semaphore_wait(barrier, 21)

    a1 = [
        [
            go(
                to_kv(
                    q_hbm.at[:, feats(g)], qz[g].at[z], a1_s.at[g * 8 + d], a1_r.at[g * 8 + d],
                    z_peer(d),
                )
            )
            for d in FAR_FIRST
        ]
        for g in groups
    ]

    slots = k_ref.shape[0]
    pages = slots // PAGE
    blocks = pages // ROWS
    lane_page = lax.broadcasted_iota(jnp.int32, (pages, slots), 1) // PAGE
    on_page = lane_page == lax.broadcasted_iota(jnp.int32, (pages, slots), 0)
    small[0].wait()
    request_row = jnp.broadcast_to(sr_ref[...].reshape(1, slots).astype(F32), (pages, slots))
    page_request = jnp.max(jnp.where(on_page, request_row, -1.0), axis=1, keepdims=True)
    idc[b] = jnp.broadcast_to(page_request, (pages, 128))
    ids = [go(to_kv(idc.at[b], idc.at[b], id_s.at[e], id_r.at[e], b_peer(e))) for e in FAR_FIRST]

    for load in large:
        load.start()

    def weights_x(first, last):
        part = pl.ds(first, last - first)
        sem = 0 if first == 0 else NX
        return [
            go(to_kv(w_hbm.at[part], wg.at[b, part], w_s.at[sem + d], w_r.at[sem + d], x_peer(d)))
            for d in (2, 1, 3)
        ]

    def weights_on(copies, first, last):
        part = pl.ds(first, last - first)
        sem = 0 if first == 0 else NX
        done = []
        for copy, d in zip(copies, (2, 1, 3)):
            arrive(copy)
            block = wg.at[lax.rem(x + NX - d, NX) * 2 + c, part]
            done.append(go(to_kv(block, block, f_s.at[sem + d], f_r.at[sem + d], sibling)))
        return done

    chunks = wg.shape[1]
    early = weights_x(0, EARLY)
    weight_own = go(to_kv(w_hbm, wg.at[b], w_s.at[0], w_r.at[0], sibling))

    for load in small[1:]:
        load.wait()
    live_row = jnp.broadcast_to(sv_ref[...].reshape(1, slots), (pages, slots))
    live = jnp.where(on_page, live_row, 0) == 1
    lane8 = lax.broadcasted_iota(jnp.int32, (ROWS, 128), 1)
    for g, (first, heads) in enumerate(GROUPS):
        own = jnp.zeros((ROWS, 128), F32)
        for h in range(heads):
            new_key = nk_ref[:, head_at(first + h)].astype(F32)
            product = qz[g][z, :, head_at(h)].astype(F32) * new_key
            own = jnp.where(lane8 == h, jnp.sum(product, axis=1, keepdims=True) * SCALE, own)
        sb[g][:, : heads * HD] = nv_ref[:, feats(g)]
        sb[g][:, heads * HD :] = split3(own).astype(BF16)
        ob[g][:, blocks:] = jnp.zeros((NB, ob[g].shape[1] - blocks) + ob[g].shape[2:], BF16)

    a2 = []
    for g, (first, heads) in enumerate(GROUPS):
        if g == 0:
            arrive(*ids)
            lane_q = lax.broadcasted_iota(jnp.int32, (NB * pages, NZ * ROWS), 1)
            place = (lane_q // ROWS) * 16 + lax.rem(lane_q, ROWS)
            lane_request = (x * 128 + c * ROWS + place).astype(F32)
            wanted = idc[...].reshape(NB * pages, 128)[:, : NZ * ROWS]
            pick = jnp.where(wanted == lane_request, 1.0, 0.0).astype(BF16)
        arrive(*a1[g])
        line = qz[g][...].astype(F32).reshape(NZ * ROWS, heads * HD).astype(BF16)
        picked = jnp.dot(pick, line, preferred_element_type=F32)
        qs[g][...] = picked.reshape(NB, blocks, ROWS, heads * HD).astype(BF16)
        a2.append(
            [
                go(
                    to_kv(
                        qs[g].at[b_at(e)], qr[g].at[b], a2_s.at[g * 8 + e], a2_r.at[g * 8 + e],
                        b_peer(e),
                    )
                )
                for e in FAR_FIRST
            ]
        )
        qr[g][b] = qs[g][b]

    large[1].wait()
    large[2].wait()
    lane24 = lax.broadcasted_iota(jnp.int32, (pages, 128), 1)
    b1 = []
    for g, (first, heads) in enumerate(GROUPS):
        arrive(*a2[g])
        queries = jnp.sum(qr[g][...].astype(F32), axis=0).reshape(pages, heads * HD).astype(BF16)
        scores = [
            lax.dot_general(
                queries[:, head_at(h)], k_ref[:, head_at(first + h)], (((1,), (1,)), ((), ())),
                preferred_element_type=F32,
            )
            for h in range(heads)
        ]
        scores = [jnp.where(live, SCALE * score, FLOOR) for score in scores]
        top = [jnp.max(score, axis=1, keepdims=True) for score in scores]
        weights = [
            jnp.where(live, jnp.exp(score - high), 0.0).astype(BF16)
            for score, high in zip(scores, top)
        ]
        total = [jnp.sum(weight.astype(F32), axis=1, keepdims=True) for weight in weights]
        parts = [
            jnp.dot(weights[h], v_ref[:, head_at(first + h)], preferred_element_type=F32)
            for h in range(heads)
        ]
        tops = jnp.zeros((pages, 128), F32)
        for h in range(heads):
            part = (parts[h] / total[h]).reshape(blocks, ROWS, HD)
            ob[g][b, :blocks, :, head_at(h)] = part.astype(BF16)
            tops = jnp.where(lane24 == h, top[h] + jnp.log(total[h]), tops)
        stats = split3(tops)
        if g == 0:
            request_high = jnp.floor(page_request * 0.125)
            stats = jnp.where(lane24 == 24, request_high + 1.0, stats)
            stats = jnp.where(lane24 == 25, page_request - 8.0 * request_high, stats)
        stats = stats.reshape(blocks, ROWS, 128).astype(BF16)
        ob[g][b, :blocks, :, heads * HD :] = stats
        mine = ob[g].at[b, pl.ds(0, blocks)]
        b1.append(
            [
                go(to_kv(mine, mine, b1_s.at[g * 8 + e], b1_r.at[g * 8 + e], b_peer(e)))
                for e in FAR_FIRST
            ]
        )
    self_copies = [
        go(to_kv(sb[g], rb[g].at[NZ], self_s.at[g], self_r.at[g], owner)) for g in groups
    ]
    early_on = weights_on(early, 0, EARLY)

    depth = NB * ob[0].shape[1] * ROWS
    count = NZ * ROWS
    lane64 = lax.broadcasted_iota(jnp.int32, (count, 128), 1)
    b2 = []
    for g, (first, heads) in enumerate(GROUPS):
        arrive(*b1[g])
        turned = ob[g][:, :, :, heads * HD :].astype(F32).reshape(depth, 128).T
        row_top = turned[0:8] + turned[8:16] + turned[16:24]
        if g == 0:
            row_request = turned[24:25] * 8.0 + turned[25:26]
            row_q = lax.broadcasted_iota(jnp.int32, (count, depth), 0)
            my_request = (
                lax.rem(row_q // ROWS + 4, NZ) * 64 + b * ROWS + lax.rem(row_q, ROWS) + 8
            ).astype(F32)
            match = jnp.broadcast_to(row_request, (count, depth)) == my_request
        tops = jnp.full((count, 128), FLOOR, F32)
        for h in range(heads):
            level = jnp.where(match, jnp.broadcast_to(row_top[h : h + 1], (count, depth)), FLOOR)
            top = jnp.max(level, axis=1, keepdims=True)
            weight = jnp.where(match, jnp.exp(level - top), 0.0).astype(BF16)
            total = jnp.sum(weight.astype(F32), axis=1, keepdims=True)
            rows = ob[g][:, :, :, head_at(h)].astype(F32).reshape(depth, HD).astype(BF16)
            some = total > 0.0
            safe = jnp.where(some, total, 1.0)
            part = jnp.dot(weight, rows, preferred_element_type=F32) / safe
            cb[g][:, :, head_at(h)] = part.reshape(NZ, ROWS, HD).astype(BF16)
            tops = jnp.where(lane64 == h, jnp.where(some, top + jnp.log(safe), FLOOR), tops)
        cb[g][:, :, heads * HD :] = split3(tops).reshape(NZ, ROWS, 128).astype(BF16)
        b2.append(
            [
                go(
                    to_kv(
                        cb[g].at[z_at(d)], rb[g].at[z], b2_s.at[g * 8 + d], b2_r.at[g * 8 + d],
                        z_peer(d),
                    )
                )
                for d in FAR_FIRST
            ]
        )
        rb[g][z] = cb[g][z]
    late = weights_x(EARLY, chunks)

    b3 = []
    for g, (first, heads) in enumerate(GROUPS):
        arrive(*b2[g], self_copies[g])
        level = join3(rb[g][:, :, heads * HD :].astype(F32))
        share = jnp.exp(level - jnp.max(level, axis=0, keepdims=True))
        share = share / jnp.sum(share, axis=0, keepdims=True)
        for h in range(heads):
            part = share[:, :, h : h + 1] * rb[g][:, :, head_at(h)].astype(F32)
            az[g][z, :, head_at(h)] = jnp.sum(part, axis=0).astype(BF16)
        b3.append(
            [
                go(to_kv(az[g].at[z], az[g].at[z], b3_s.at[g * 8 + d], b3_r.at[g * 8 + d], z_peer(d)))
                for d in FAR_FIRST
            ]
        )
    late_on = weights_on(late, EARLY, chunks)
    large[0].wait()

    columns = chunks * 16

    def attended(g):
        arrive(*b3[g])
        return az[g][...].astype(F32).reshape(count, GROUPS[g][1] * HD).astype(BF16)

    def product(rows, e, g):
        block = wg[b_at(e)].reshape(columns, FEAT)[:, feats(g).start : feats(g).start + feats(g).size]
        return lax.dot_general(
            rows, block, (((1,), (1,)), ((), ())), preferred_element_type=F32
        )

    rows = attended(0)
    arrive(weight_own, *early_on, *late_on)
    for e in FAR_FIRST + (0,):
        acc[e, :, :columns] = product(rows, e, 0)
    rows = attended(1)
    c1 = []
    for e in FAR_FIRST + (0,):
        block = acc[e, :, :columns] + product(rows, e, 1)
        pc[e, :, :, :columns] = block.reshape(NZ, ROWS, columns).astype(BF16)
        for d in FAR_FIRST + (0,):
            band = lax.rem(t + d + 4, NT)
            if d == 0 and e == 0:
                fr[t * NB + b] = pc[e, band]
                continue
            pltpu.make_async_remote_copy(
                src_ref=pc.at[e, band], dst_ref=fr.at[t * NB + b], send_sem=c_s, recv_sem=c_r,
                device_id={"kv": b_peer(e), "tp": lax.rem(t + d, NT)}, device_id_type=MESH,
            ).start()
    for copy in sends:
        copy.wait_send()
    others = fr.at[pl.ds(0, NT * NB - 1)]
    every = to_kv(others, others, c_s, c_r, sibling)
    every.wait_recv()
    out_ref[...] = jnp.sum(fr[...].astype(F32).reshape(NT, NB * ROWS, 128), axis=0)
    every.wait_send()


def on_device(
    queries,
    new_keys,
    new_values,
    keys,
    values,
    slot_request,
    slot_valid,
    out_weight,
    out_bias,
    residual,
):
    slots = keys.shape[0]
    columns = out_weight.shape[1]
    pages = slots // PAGE
    blocks = pages // ROWS
    padded = 4
    vmem = pl.BlockSpec(memory_space=pltpu.VMEM)
    hbm = pl.BlockSpec(memory_space=pltpu.HBM)
    dma = pltpu.SemaphoreType.DMA

    def grouped(*lead, stats):
        return [
            pltpu.VMEM(lead + (heads * HD + (128 if stats else 0),), BF16) for _, heads in GROUPS
        ]

    projected = pl.pallas_call(
        kernel,
        out_shape=jax.ShapeDtypeStruct((NB * ROWS, 128), F32),
        in_specs=[hbm] * 8,
        out_specs=vmem,
        scratch_shapes=[
            pltpu.VMEM((ROWS, FEAT), BF16),
            pltpu.VMEM((ROWS, FEAT), BF16),
            pltpu.VMEM((slots,), jnp.int32),
            pltpu.VMEM((slots,), jnp.int32),
            pltpu.VMEM((slots, FEAT), BF16),
            pltpu.VMEM((slots, FEAT), BF16),
            pltpu.VMEM((NB, columns // 16, 16, FEAT), BF16),
            pltpu.VMEM((NB, pages, 128), F32),
            grouped(NZ, ROWS, stats=False),
            grouped(NB, blocks, ROWS, stats=False),
            grouped(NB, blocks, ROWS, stats=False),
            grouped(NB, padded, ROWS, stats=True),
            grouped(NZ, ROWS, stats=True),
            grouped(NZ + 1, ROWS, stats=True),
            grouped(ROWS, stats=True),
            grouped(NZ, ROWS, stats=False),
            pltpu.VMEM((NB, NZ * ROWS, 128), F32),
            pltpu.VMEM((NB, NZ, ROWS, 128), BF16),
            pltpu.VMEM((NT * NB, ROWS, 128), BF16),
            dma((9,)),
            dma((2 * NX,)), dma((2 * NX,)), dma((2 * NX,)), dma((2 * NX,)),
            dma((NB,)), dma((NB,)),
        ]
        + [dma((16,))] * 10
        + [dma((2,)), dma((2,)), dma, dma],
        compiler_params=pltpu.CompilerParams(
            collective_id=0, has_side_effects=True, vmem_limit_bytes=GRANT
        ),
        name="paged_decode",
    )(
        queries, new_keys, new_values, slot_request, slot_valid, keys, values,
        out_weight.T.reshape(columns // 16, 16, FEAT),
    )
    total = (
        residual.astype(F32) + projected[:, :columns] + out_bias.astype(F32)[None, :]
    )
    return total.astype(BF16)


def solution(mesh):
    placed = (
        P("kv", "tp"),
        P("kv", "tp"),
        P("kv", "tp"),
        P("kv", "tp"),
        P("kv", "tp"),
        P("kv"),
        P("kv"),
        P("tp", "kv"),
        P("kv"),
        P("tp", "kv"),
    )
    return jax.shard_map(
        on_device, mesh=mesh, in_specs=placed, out_specs=P("tp", "kv"), check_vma=False
    )
```

```python
import math

import jax
import jax.numpy as jnp
from jax import lax
from jax.experimental import pallas as pl
from jax.experimental.pallas import tpu as pltpu
from jax.sharding import PartitionSpec as P

HD = 128
HEADS = 7
FEAT = HEADS * HD
PAGE = 16
NX, NZ, NT, NB = 4, 8, 8, 8
ROWS = 8
FLOOR = -1e30
SCALE = 1.0 / math.sqrt(HD)
MESH = pl.DeviceIdType.MESH
F32, BF16 = jnp.float32, jnp.bfloat16

GROUPS = ((0, 4), (4, 3))

FAR_FIRST = (4, 3, 5, 2, 6, 1, 7)
X_FIRST = (2, 1, 3)

EARLY = 3

GRANT = 63 << 20


def kv_of(x, z, c):
    return (x * NZ + z) * 2 + c


def head_at(h):
    return slice(h * HD, (h + 1) * HD)


def split3(tile):
    lane = lax.broadcasted_iota(jnp.int32, tile.shape, 1)
    tile = jnp.where(lane < 8, tile, 0.0)
    high = tile.astype(BF16).astype(F32)
    middle = (tile - high).astype(BF16).astype(F32)
    low = tile - high - middle
    return high + pltpu.roll(middle, 8, 1) + pltpu.roll(low, 16, 1)


def join3(tile):
    axis = tile.ndim - 1
    return tile + pltpu.roll(tile, 128 - 8, axis) + pltpu.roll(tile, 128 - 16, axis)


def kernel(
    q_hbm, nk_hbm, nv_hbm, sr_hbm, sv_hbm, k_hbm, v_hbm, w_hbm, bias_hbm, out_ref,
    bias_ref, nk_ref, nv_ref, sr_ref, sv_ref, k_ref, v_ref, wg, idc, qz, qs, qr, ob, cb, rb, sb, az,
    acc, pc, fr, local, w_s, w_r, f_s, f_r, l_s, l_r, id_s, id_r, a1_s, a1_r, a2_s, a2_r, b1_s, b1_r,
    b2_s, b2_r, b3_s, b3_r, self_s, self_r, c_s, c_r,
):
    k = lax.axis_index("kv")
    t = lax.axis_index("tp")
    c = lax.rem(k, 2)
    xz = k // 2
    x = xz // NZ
    z = lax.rem(xz, NZ)
    b = x * 2 + c

    def to_kv(src, dst, send, recv, kv):
        return pltpu.make_async_remote_copy(
            src_ref=src, dst_ref=dst, send_sem=send, recv_sem=recv,
            device_id={"kv": kv}, device_id_type=MESH,
        )

    def z_at(d):
        return lax.rem(z + d, NZ)

    def b_at(e):
        return lax.rem(b + e, NB)

    def z_peer(d):
        return kv_of(x, z_at(d), c)

    def b_peer(e):
        other = b_at(e)
        return kv_of(other // 2, z, lax.rem(other, 2))

    def x_peer(d):
        return kv_of(lax.rem(x + d, NX), z, c)

    sibling = kv_of(x, z, 1 - c)
    owner = kv_of(lax.rem(z, 4), lax.rem(2 * x + z // 4 + 4, NZ), c)

    barrier = pltpu.get_barrier_semaphore()
    for d in FAR_FIRST:
        pl.semaphore_signal(barrier, inc=1, device_id={"kv": z_peer(d)}, device_id_type=MESH)
    for d in range(1, NX):
        pl.semaphore_signal(barrier, inc=1, device_id={"kv": x_peer(d)}, device_id_type=MESH)
    pl.semaphore_signal(barrier, inc=1, device_id={"kv": sibling}, device_id_type=MESH)
    for d in FAR_FIRST:
        pl.semaphore_signal(
            barrier, inc=1, device_id={"tp": lax.rem(t + d, NT)}, device_id_type=MESH
        )

    def feats(g):
        first, heads = GROUPS[g]
        return pl.ds(first * HD, heads * HD)

    groups = range(len(GROUPS))
    small = [
        pltpu.make_async_copy(sr_hbm, sr_ref, local.at[0]),
        pltpu.make_async_copy(sv_hbm, sv_ref, local.at[1]),
        pltpu.make_async_copy(nk_hbm, nk_ref, local.at[2]),
        pltpu.make_async_copy(nv_hbm, nv_ref, local.at[3]),
        pltpu.make_async_copy(bias_hbm, bias_ref, local.at[9]),
    ] + [
        pltpu.make_async_copy(q_hbm.at[:, feats(g)], qz[g].at[c, z], local.at[4 + g]) for g in groups
    ]
    large = [
        pltpu.make_async_copy(w_hbm, wg.at[b], local.at[6]),
        pltpu.make_async_copy(k_hbm, k_ref, local.at[7]),
        pltpu.make_async_copy(v_hbm, v_ref, local.at[8]),
    ]
    for load in small:
        load.start()

    sends = []

    def go(copy):
        copy.start()
        sends.append(copy)
        return copy

    def arrive(*copies):
        for copy in copies:
            copy.wait_recv()

    pl.semaphore_wait(barrier, 18)

    a1 = [
        [
            go(
                to_kv(
                    q_hbm.at[:, feats(g)], qz[g].at[c, z], a1_s.at[g * 8 + d], a1_r.at[g * 8 + d],
                    z_peer(d),
                )
            )
            for d in FAR_FIRST
        ]
        for g in groups
    ]

    slots = k_ref.shape[0]
    pages = slots // PAGE
    blocks = pages // ROWS
    lane_page = lax.broadcasted_iota(jnp.int32, (pages, slots), 1) // PAGE
    on_page = lane_page == lax.broadcasted_iota(jnp.int32, (pages, slots), 0)
    small[0].wait()
    request_row = jnp.broadcast_to(sr_ref[...].reshape(1, slots).astype(F32), (pages, slots))
    page_request = jnp.max(jnp.where(on_page, request_row, -1.0), axis=1, keepdims=True)
    idc[x] = jnp.broadcast_to(page_request, (pages, 128))
    ids = [go(to_kv(idc.at[x], idc.at[x], id_s.at[d], id_r.at[d], x_peer(d))) for d in X_FIRST]

    for load in large:
        load.start()

    def weights_x(first, last):
        part = pl.ds(first, last - first)
        sem = 0 if first == 0 else NX
        return [
            go(to_kv(w_hbm.at[part], wg.at[b, part], w_s.at[sem + d], w_r.at[sem + d], x_peer(d)))
            for d in X_FIRST
        ]

    def weights_on(copies, first, last):
        part = pl.ds(first, last - first)
        sem = 0 if first == 0 else NX
        done = []
        for copy, d in zip(copies, X_FIRST):
            arrive(copy)
            block = wg.at[lax.rem(x + NX - d, NX) * 2 + c, part]
            done.append(go(to_kv(block, block, f_s.at[sem + d], f_r.at[sem + d], sibling)))
        return done

    chunks = wg.shape[1]
    early = weights_x(0, EARLY)
    weight_own = go(to_kv(w_hbm, wg.at[b], w_s.at[0], w_r.at[0], sibling))

    for load in small[1:]:
        load.wait()
    live_row = jnp.broadcast_to(sv_ref[...].reshape(1, slots), (pages, slots))
    live = jnp.where(on_page, live_row, 0) == 1
    lane8 = lax.broadcasted_iota(jnp.int32, (ROWS, 128), 1)
    for g, (first, heads) in enumerate(GROUPS):
        own = jnp.zeros((ROWS, 128), F32)
        for h in range(heads):
            new_key = nk_ref[:, head_at(first + h)].astype(F32)
            product = qz[g][c, z, :, head_at(h)].astype(F32) * new_key
            own = jnp.where(lane8 == h, jnp.sum(product, axis=1, keepdims=True) * SCALE, own)
        sb[g][:, : heads * HD] = nv_ref[:, feats(g)]
        sb[g][:, heads * HD :] = split3(own).astype(BF16)
        ob[g][:, blocks:] = jnp.zeros((NB, ob[g].shape[1] - blocks) + ob[g].shape[2:], BF16)

    line_copies = []
    for g in groups:
        arrive(*a1[g])
        line = qz[g].at[c]
        line_copies.append(go(to_kv(line, line, l_s.at[g], l_r.at[g], sibling)))
    arrive(*ids)
    lane_q = lax.broadcasted_iota(jnp.int32, (NX * pages, 2 * NZ * ROWS), 1)
    core = lane_q // (NZ * ROWS)
    place = lax.rem(lane_q // ROWS, NZ) * 16 + core * ROWS + lax.rem(lane_q, ROWS)
    wanted = idc[...].reshape(NX * pages, 128)
    pick = jnp.where(wanted == (x * 128 + place).astype(F32), 1.0, 0.0).astype(BF16)
    a2 = []
    for g, (first, heads) in enumerate(GROUPS):
        arrive(line_copies[g])
        line = qz[g][...].astype(F32).reshape(2 * NZ * ROWS, heads * HD).astype(BF16)
        picked = jnp.dot(pick, line, preferred_element_type=F32)
        qs[g][...] = picked.reshape(NX, blocks, ROWS, heads * HD).astype(BF16)
        a2.append(
            [
                go(
                    to_kv(
                        qs[g].at[lax.rem(x + d, NX)], qr[g].at[x], a2_s.at[g * 8 + d],
                        a2_r.at[g * 8 + d], x_peer(d),
                    )
                )
                for d in X_FIRST
            ]
        )
        qr[g][x] = qs[g][x]

    large[1].wait()
    large[2].wait()
    lane24 = lax.broadcasted_iota(jnp.int32, (pages, 128), 1)
    b1, both = [], []
    for g, (first, heads) in enumerate(GROUPS):
        arrive(*a2[g])
        queries = jnp.sum(qr[g][...].astype(F32), axis=0).reshape(pages, heads * HD).astype(BF16)
        scores = [
            lax.dot_general(
                queries[:, head_at(h)], k_ref[:, head_at(first + h)], (((1,), (1,)), ((), ())),
                preferred_element_type=F32,
            )
            for h in range(heads)
        ]
        scores = [jnp.where(live, SCALE * score, FLOOR) for score in scores]
        top = [jnp.max(score, axis=1, keepdims=True) for score in scores]
        weights = [
            jnp.where(live, jnp.exp(score - high), 0.0).astype(BF16)
            for score, high in zip(scores, top)
        ]
        total = [jnp.sum(weight.astype(F32), axis=1, keepdims=True) for weight in weights]
        parts = [
            jnp.dot(weights[h], v_ref[:, head_at(first + h)], preferred_element_type=F32)
            for h in range(heads)
        ]
        tops = jnp.zeros((pages, 128), F32)
        for h in range(heads):
            part = (parts[h] / total[h]).reshape(blocks, ROWS, HD)
            ob[g][b, :blocks, :, head_at(h)] = part.astype(BF16)
            tops = jnp.where(lane24 == h, top[h] + jnp.log(total[h]), tops)
        stats = split3(tops)
        if g == 0:
            request_high = jnp.floor(page_request * 0.125)
            stats = jnp.where(lane24 == 24, request_high + 1.0, stats)
            stats = jnp.where(lane24 == 25, page_request - 8.0 * request_high, stats)
        stats = stats.reshape(blocks, ROWS, 128).astype(BF16)
        ob[g][b, :blocks, :, heads * HD :] = stats
        mine = ob[g].at[b, pl.ds(0, blocks)]
        b1.append(
            [
                go(to_kv(mine, mine, b1_s.at[g * 8 + d], b1_r.at[g * 8 + d], x_peer(d)))
                for d in X_FIRST
            ]
        )
        both.append([go(to_kv(mine, mine, b1_s.at[g * 8 + 4], b1_r.at[g * 8 + 4], sibling))])
    self_copies = [
        go(to_kv(sb[g], rb[g].at[NZ], self_s.at[g], self_r.at[g], owner)) for g in groups
    ]
    early_on = weights_on(early, 0, EARLY)

    for g in groups:
        for copy, d in zip(b1[g], X_FIRST):
            arrive(copy)
            block = ob[g].at[lax.rem(x + NX - d, NX) * 2 + c, pl.ds(0, blocks)]
            sem = g * 8 + 4 + d
            both[g].append(go(to_kv(block, block, b1_s.at[sem], b1_r.at[sem], sibling)))
    late = weights_x(EARLY, chunks)

    depth = NB * ob[0].shape[1] * ROWS
    count = NZ * ROWS
    lane64 = lax.broadcasted_iota(jnp.int32, (count, 128), 1)
    b2 = []
    for g, (first, heads) in enumerate(GROUPS):
        arrive(*both[g])
        turned = ob[g][:, :, :, heads * HD :].astype(F32).reshape(depth, 128).T
        row_top = turned[0:8] + turned[8:16] + turned[16:24]
        if g == 0:
            row_request = turned[24:25] * 8.0 + turned[25:26]
            row_q = lax.broadcasted_iota(jnp.int32, (count, depth), 0)
            my_request = (
                lax.rem(row_q // ROWS + 4, NZ) * 64 + b * ROWS + lax.rem(row_q, ROWS) + 8
            ).astype(F32)
            match = jnp.broadcast_to(row_request, (count, depth)) == my_request
        tops = jnp.full((count, 128), FLOOR, F32)
        for h in range(heads):
            level = jnp.where(match, jnp.broadcast_to(row_top[h : h + 1], (count, depth)), FLOOR)
            top = jnp.max(level, axis=1, keepdims=True)
            weight = jnp.where(match, jnp.exp(level - top), 0.0).astype(BF16)
            total = jnp.sum(weight.astype(F32), axis=1, keepdims=True)
            rows = ob[g][:, :, :, head_at(h)].astype(F32).reshape(depth, HD).astype(BF16)
            some = total > 0.0
            safe = jnp.where(some, total, 1.0)
            part = jnp.dot(weight, rows, preferred_element_type=F32) / safe
            cb[g][:, :, head_at(h)] = part.reshape(NZ, ROWS, HD).astype(BF16)
            tops = jnp.where(lane64 == h, jnp.where(some, top + jnp.log(safe), FLOOR), tops)
        cb[g][:, :, heads * HD :] = split3(tops).reshape(NZ, ROWS, 128).astype(BF16)
        b2.append(
            [
                go(
                    to_kv(
                        cb[g].at[z_at(d)], rb[g].at[z], b2_s.at[g * 8 + d], b2_r.at[g * 8 + d],
                        z_peer(d),
                    )
                )
                for d in FAR_FIRST
            ]
        )
        rb[g][z] = cb[g][z]

    b3 = []
    for g, (first, heads) in enumerate(GROUPS):
        arrive(*b2[g], self_copies[g])
        level = join3(rb[g][:, :, heads * HD :].astype(F32))
        share = jnp.exp(level - jnp.max(level, axis=0, keepdims=True))
        share = share / jnp.sum(share, axis=0, keepdims=True)
        for h in range(heads):
            part = share[:, :, h : h + 1] * rb[g][:, :, head_at(h)].astype(F32)
            az[g][z, :, head_at(h)] = jnp.sum(part, axis=0).astype(BF16)
        b3.append(
            [
                go(to_kv(az[g].at[z], az[g].at[z], b3_s.at[g * 8 + d], b3_r.at[g * 8 + d], z_peer(d)))
                for d in FAR_FIRST
            ]
        )
    late_on = weights_on(late, EARLY, chunks)
    large[0].wait()

    columns = chunks * 16

    def attended(g):
        arrive(*b3[g])
        return az[g][...].astype(F32).reshape(count, GROUPS[g][1] * HD).astype(BF16)

    def product(rows, e, g):
        block = wg[b_at(e)].reshape(columns, FEAT)[:, feats(g).start : feats(g).start + feats(g).size]
        return lax.dot_general(
            rows, block, (((1,), (1,)), ((), ())), preferred_element_type=F32
        )

    rows = attended(0)
    arrive(weight_own, *early_on, *late_on)
    for e in FAR_FIRST + (0,):
        acc[e, :, :columns] = product(rows, e, 0)
    rows = attended(1)
    c1 = []
    for e in FAR_FIRST + (0,):
        block = acc[e, :, :columns] + product(rows, e, 1)
        pc[e, :, :, :columns] = block.reshape(NZ, ROWS, columns).astype(BF16)
        for d in FAR_FIRST + (0,):
            band = lax.rem(t + d + 4, NT)
            if d == 0 and e == 0:
                fr[t * NB + b] = pc[e, band]
                continue
            pltpu.make_async_remote_copy(
                src_ref=pc.at[e, band], dst_ref=fr.at[t * NB + b], send_sem=c_s, recv_sem=c_r,
                device_id={"kv": b_peer(e), "tp": lax.rem(t + d, NT)}, device_id_type=MESH,
            ).start()
    for copy in sends:
        copy.wait_send()
    others = fr.at[pl.ds(0, NT * NB - 1)]
    every = to_kv(others, others, c_s, c_r, sibling)
    every.wait_recv()
    summed = jnp.sum(fr[...].astype(F32).reshape(NT, NB * ROWS, 128), axis=0)
    out_ref[:, :columns] = summed[:, :columns] + bias_ref[...].astype(F32).reshape(1, columns)
    every.wait_send()


def on_device(
    queries,
    new_keys,
    new_values,
    keys,
    values,
    slot_request,
    slot_valid,
    out_weight,
    out_bias,
    residual,
):
    slots = keys.shape[0]
    columns = out_weight.shape[1]
    pages = slots // PAGE
    blocks = pages // ROWS
    padded = 4
    vmem = pl.BlockSpec(memory_space=pltpu.VMEM)
    hbm = pl.BlockSpec(memory_space=pltpu.HBM)
    dma = pltpu.SemaphoreType.DMA

    def grouped(*lead, stats):
        return [
            pltpu.VMEM(lead + (heads * HD + (128 if stats else 0),), BF16) for _, heads in GROUPS
        ]

    projected = pl.pallas_call(
        kernel,
        out_shape=jax.ShapeDtypeStruct((NB * ROWS, 128), F32),
        in_specs=[hbm] * 9,
        out_specs=vmem,
        scratch_shapes=[
            pltpu.VMEM((columns,), BF16),
            pltpu.VMEM((ROWS, FEAT), BF16),
            pltpu.VMEM((ROWS, FEAT), BF16),
            pltpu.VMEM((slots,), jnp.int32),
            pltpu.VMEM((slots,), jnp.int32),
            pltpu.VMEM((slots, FEAT), BF16),
            pltpu.VMEM((slots, FEAT), BF16),
            pltpu.VMEM((NB, columns // 16, 16, FEAT), BF16),
            pltpu.VMEM((NX, pages, 128), F32),
            grouped(2, NZ, ROWS, stats=False),
            grouped(NX, blocks, ROWS, stats=False),
            grouped(NX, blocks, ROWS, stats=False),
            grouped(NB, padded, ROWS, stats=True),
            grouped(NZ, ROWS, stats=True),
            grouped(NZ + 1, ROWS, stats=True),
            grouped(ROWS, stats=True),
            grouped(NZ, ROWS, stats=False),
            pltpu.VMEM((NB, NZ * ROWS, 128), F32),
            pltpu.VMEM((NB, NZ, ROWS, 128), BF16),
            pltpu.VMEM((NT * NB, ROWS, 128), BF16),
            dma((10,)),
            dma((2 * NX,)), dma((2 * NX,)), dma((2 * NX,)), dma((2 * NX,)),
            dma((2,)), dma((2,)), dma((NX,)), dma((NX,)),
        ]
        + [dma((16,))] * 10
        + [dma((2,)), dma((2,)), dma, dma],
        compiler_params=pltpu.CompilerParams(
            collective_id=0, has_side_effects=True, vmem_limit_bytes=GRANT
        ),
        name="paged_decode",
    )(
        queries, new_keys, new_values, slot_request, slot_valid, keys, values,
        out_weight.T.reshape(columns // 16, 16, FEAT), out_bias,
    )
    total = residual.astype(F32) + projected[:, :columns]
    return total.astype(BF16)


def solution(mesh):
    placed = (
        P("kv", "tp"),
        P("kv", "tp"),
        P("kv", "tp"),
        P("kv", "tp"),
        P("kv", "tp"),
        P("kv"),
        P("kv"),
        P("tp", "kv"),
        P("kv"),
        P("tp", "kv"),
    )
    return jax.shard_map(
        on_device, mesh=mesh, in_specs=placed, out_specs=P("tp", "kv"), check_vma=False
    )
```

```python
import math

import jax
import jax.numpy as jnp
from jax import lax
from jax.experimental import pallas as pl
from jax.experimental.pallas import tpu as pltpu
from jax.sharding import PartitionSpec as P

HD = 128
HEADS = 7
FEAT = HEADS * HD
PAGE = 16
NX, NZ, NT, NB = 4, 8, 8, 8
ROWS = 8
FLOOR = -1e30
SCALE = 1.0 / math.sqrt(HD)
MESH = pl.DeviceIdType.MESH
F32, BF16 = jnp.float32, jnp.bfloat16

GROUPS = ((0, 3), (3, 4))

FAR_FIRST = (4, 3, 5, 2, 6, 1, 7)
X_FIRST = (2, 1, 3)

EARLY = 3

GRANT = 63 << 20


def kv_of(x, z, c):
    return (x * NZ + z) * 2 + c


def head_at(h):
    return slice(h * HD, (h + 1) * HD)


def split3(tile):
    lane = lax.broadcasted_iota(jnp.int32, tile.shape, 1)
    tile = jnp.where(lane < 8, tile, 0.0)
    high = tile.astype(BF16).astype(F32)
    middle = (tile - high).astype(BF16).astype(F32)
    low = tile - high - middle
    return high + pltpu.roll(middle, 8, 1) + pltpu.roll(low, 16, 1)


def join3(tile):
    axis = tile.ndim - 1
    return tile + pltpu.roll(tile, 128 - 8, axis) + pltpu.roll(tile, 128 - 16, axis)


def kernel(
    q_hbm, nk_hbm, nv_hbm, sr_hbm, sv_hbm, k_hbm, v_hbm, w_hbm, bias_hbm, out_ref,
    bias_ref, nk_ref, nv_ref, sr_ref, sv_ref, k_ref, v_ref, wg, idc, qz, qs, qr, ob, cb, rb, sb, az,
    acc, pc, fr, local, w_s, w_r, f_s, f_r, l_s, l_r, id_s, id_r, a1_s, a1_r, a2_s, a2_r, b1_s, b1_r,
    b2_s, b2_r, b3_s, b3_r, self_s, self_r, c_s, c_r,
):
    k = lax.axis_index("kv")
    t = lax.axis_index("tp")
    c = lax.rem(k, 2)
    xz = k // 2
    x = xz // NZ
    z = lax.rem(xz, NZ)
    b = x * 2 + c

    def to_kv(src, dst, send, recv, kv):
        return pltpu.make_async_remote_copy(
            src_ref=src, dst_ref=dst, send_sem=send, recv_sem=recv,
            device_id={"kv": kv}, device_id_type=MESH,
        )

    def z_at(d):
        return lax.rem(z + d, NZ)

    def b_at(e):
        return lax.rem(b + e, NB)

    def z_peer(d):
        return kv_of(x, z_at(d), c)

    def b_peer(e):
        other = b_at(e)
        return kv_of(other // 2, z, lax.rem(other, 2))

    def x_peer(d):
        return kv_of(lax.rem(x + d, NX), z, c)

    sibling = kv_of(x, z, 1 - c)
    owner = kv_of(lax.rem(z, 4), lax.rem(2 * x + z // 4 + 4, NZ), c)

    barrier = pltpu.get_barrier_semaphore()
    for d in FAR_FIRST:
        pl.semaphore_signal(barrier, inc=1, device_id={"kv": z_peer(d)}, device_id_type=MESH)
    for d in range(1, NX):
        pl.semaphore_signal(barrier, inc=1, device_id={"kv": x_peer(d)}, device_id_type=MESH)
    pl.semaphore_signal(barrier, inc=1, device_id={"kv": sibling}, device_id_type=MESH)
    for d in FAR_FIRST:
        pl.semaphore_signal(
            barrier, inc=1, device_id={"tp": lax.rem(t + d, NT)}, device_id_type=MESH
        )

    def feats(g):
        first, heads = GROUPS[g]
        return pl.ds(first * HD, heads * HD)

    groups = range(len(GROUPS))
    small = [
        pltpu.make_async_copy(sr_hbm, sr_ref, local.at[0]),
        pltpu.make_async_copy(sv_hbm, sv_ref, local.at[1]),
        pltpu.make_async_copy(nk_hbm, nk_ref, local.at[2]),
        pltpu.make_async_copy(nv_hbm, nv_ref, local.at[3]),
        pltpu.make_async_copy(bias_hbm, bias_ref, local.at[9]),
    ] + [
        pltpu.make_async_copy(q_hbm.at[:, feats(g)], qz[g].at[c, z], local.at[4 + g]) for g in groups
    ]
    large = [
        pltpu.make_async_copy(w_hbm, wg.at[b], local.at[6]),
        pltpu.make_async_copy(k_hbm, k_ref, local.at[7]),
        pltpu.make_async_copy(v_hbm, v_ref, local.at[8]),
    ]
    for load in small:
        load.start()

    sends = []

    def go(copy):
        copy.start()
        sends.append(copy)
        return copy

    def arrive(*copies):
        for copy in copies:
            copy.wait_recv()

    pl.semaphore_wait(barrier, 18)

    a1 = [
        [
            go(
                to_kv(
                    q_hbm.at[:, feats(g)], qz[g].at[c, z], a1_s.at[g * 8 + d], a1_r.at[g * 8 + d],
                    z_peer(d),
                )
            )
            for d in FAR_FIRST
        ]
        for g in groups
    ]

    slots = k_ref.shape[0]
    pages = slots // PAGE
    blocks = pages // ROWS
    lane_page = lax.broadcasted_iota(jnp.int32, (pages, slots), 1) // PAGE
    on_page = lane_page == lax.broadcasted_iota(jnp.int32, (pages, slots), 0)
    small[0].wait()
    request_row = jnp.broadcast_to(sr_ref[...].reshape(1, slots).astype(F32), (pages, slots))
    page_request = jnp.max(jnp.where(on_page, request_row, -1.0), axis=1, keepdims=True)
    idc[x] = jnp.broadcast_to(page_request, (pages, 128))
    ids = [go(to_kv(idc.at[x], idc.at[x], id_s.at[d], id_r.at[d], x_peer(d))) for d in X_FIRST]

    for load in large:
        load.start()

    def weights_x(first, last):
        part = pl.ds(first, last - first)
        sem = 0 if first == 0 else NX
        return [
            go(to_kv(w_hbm.at[part], wg.at[b, part], w_s.at[sem + d], w_r.at[sem + d], x_peer(d)))
            for d in X_FIRST
        ]

    def weights_on(copies, first, last):
        part = pl.ds(first, last - first)
        sem = 0 if first == 0 else NX
        done = []
        for copy, d in zip(copies, X_FIRST):
            arrive(copy)
            block = wg.at[lax.rem(x + NX - d, NX) * 2 + c, part]
            done.append(go(to_kv(block, block, f_s.at[sem + d], f_r.at[sem + d], sibling)))
        return done

    chunks = wg.shape[1]
    early = weights_x(0, EARLY)
    weight_own = go(to_kv(w_hbm, wg.at[b], w_s.at[0], w_r.at[0], sibling))

    for load in small[1:]:
        load.wait()
    live_row = jnp.broadcast_to(sv_ref[...].reshape(1, slots), (pages, slots))
    live = jnp.where(on_page, live_row, 0) == 1
    lane8 = lax.broadcasted_iota(jnp.int32, (ROWS, 128), 1)
    for g, (first, heads) in enumerate(GROUPS):
        own = jnp.zeros((ROWS, 128), F32)
        for h in range(heads):
            new_key = nk_ref[:, head_at(first + h)].astype(F32)
            product = qz[g][c, z, :, head_at(h)].astype(F32) * new_key
            own = jnp.where(lane8 == h, jnp.sum(product, axis=1, keepdims=True) * SCALE, own)
        sb[g][:, : heads * HD] = nv_ref[:, feats(g)]
        sb[g][:, heads * HD :] = split3(own).astype(BF16)
        ob[g][:, blocks:] = jnp.zeros((NB, ob[g].shape[1] - blocks) + ob[g].shape[2:], BF16)

    line_copies = []
    for g in groups:
        arrive(*a1[g])
        line = qz[g].at[c]
        line_copies.append(go(to_kv(line, line, l_s.at[g], l_r.at[g], sibling)))
    arrive(*ids)
    lane_q = lax.broadcasted_iota(jnp.int32, (NX * pages, 2 * NZ * ROWS), 1)
    core = lane_q // (NZ * ROWS)
    place = lax.rem(lane_q // ROWS, NZ) * 16 + core * ROWS + lax.rem(lane_q, ROWS)
    wanted = idc[...].reshape(NX * pages, 128)
    pick = jnp.where(wanted == (x * 128 + place).astype(F32), 1.0, 0.0).astype(BF16)
    a2 = []
    for g, (first, heads) in enumerate(GROUPS):
        arrive(line_copies[g])
        line = qz[g][...].astype(F32).reshape(2 * NZ * ROWS, heads * HD).astype(BF16)
        picked = jnp.dot(pick, line, preferred_element_type=F32)
        qs[g][...] = picked.reshape(NX, blocks, ROWS, heads * HD).astype(BF16)
        a2.append(
            [
                go(
                    to_kv(
                        qs[g].at[lax.rem(x + d, NX)], qr[g].at[x], a2_s.at[g * 8 + d],
                        a2_r.at[g * 8 + d], x_peer(d),
                    )
                )
                for d in X_FIRST
            ]
        )
        qr[g][x] = qs[g][x]

    large[1].wait()
    large[2].wait()
    lane24 = lax.broadcasted_iota(jnp.int32, (pages, 128), 1)
    b1, both = [], []
    for g, (first, heads) in enumerate(GROUPS):
        arrive(*a2[g])
        queries = jnp.sum(qr[g][...].astype(F32), axis=0).reshape(pages, heads * HD).astype(BF16)
        scores = [
            lax.dot_general(
                queries[:, head_at(h)], k_ref[:, head_at(first + h)], (((1,), (1,)), ((), ())),
                preferred_element_type=F32,
            )
            for h in range(heads)
        ]
        scores = [jnp.where(live, SCALE * score, FLOOR) for score in scores]
        top = [jnp.max(score, axis=1, keepdims=True) for score in scores]
        weights = [
            jnp.where(live, jnp.exp(score - high), 0.0).astype(BF16)
            for score, high in zip(scores, top)
        ]
        total = [jnp.sum(weight.astype(F32), axis=1, keepdims=True) for weight in weights]
        parts = [
            jnp.dot(weights[h], v_ref[:, head_at(first + h)], preferred_element_type=F32)
            for h in range(heads)
        ]
        tops = jnp.zeros((pages, 128), F32)
        for h in range(heads):
            part = (parts[h] / total[h]).reshape(blocks, ROWS, HD)
            ob[g][b, :blocks, :, head_at(h)] = part.astype(BF16)
            tops = jnp.where(lane24 == h, top[h] + jnp.log(total[h]), tops)
        stats = split3(tops)
        if g == 0:
            request_high = jnp.floor(page_request * 0.125)
            stats = jnp.where(lane24 == 24, request_high + 1.0, stats)
            stats = jnp.where(lane24 == 25, page_request - 8.0 * request_high, stats)
        stats = stats.reshape(blocks, ROWS, 128).astype(BF16)
        ob[g][b, :blocks, :, heads * HD :] = stats
        mine = ob[g].at[b, pl.ds(0, blocks)]
        b1.append(
            [
                go(to_kv(mine, mine, b1_s.at[g * 8 + d], b1_r.at[g * 8 + d], x_peer(d)))
                for d in X_FIRST
            ]
        )
        both.append([go(to_kv(mine, mine, b1_s.at[g * 8 + 4], b1_r.at[g * 8 + 4], sibling))])
    self_copies = [
        go(to_kv(sb[g], rb[g].at[NZ], self_s.at[g], self_r.at[g], owner)) for g in groups
    ]
    early_on = weights_on(early, 0, EARLY)

    for g in groups:
        for copy, d in zip(b1[g], X_FIRST):
            arrive(copy)
            block = ob[g].at[lax.rem(x + NX - d, NX) * 2 + c, pl.ds(0, blocks)]
            sem = g * 8 + 4 + d
            both[g].append(go(to_kv(block, block, b1_s.at[sem], b1_r.at[sem], sibling)))
    late = weights_x(EARLY, chunks)

    depth = NB * ob[0].shape[1] * ROWS
    count = NZ * ROWS
    lane64 = lax.broadcasted_iota(jnp.int32, (count, 128), 1)
    b2 = []
    for g, (first, heads) in enumerate(GROUPS):
        arrive(*both[g])
        turned = ob[g][:, :, :, heads * HD :].astype(F32).reshape(depth, 128).T
        row_top = turned[0:8] + turned[8:16] + turned[16:24]
        if g == 0:
            row_request = turned[24:25] * 8.0 + turned[25:26]
            row_q = lax.broadcasted_iota(jnp.int32, (count, depth), 0)
            my_request = (
                lax.rem(row_q // ROWS + 4, NZ) * 64 + b * ROWS + lax.rem(row_q, ROWS) + 8
            ).astype(F32)
            match = jnp.broadcast_to(row_request, (count, depth)) == my_request
        tops = jnp.full((count, 128), FLOOR, F32)
        for h in range(heads):
            level = jnp.where(match, jnp.broadcast_to(row_top[h : h + 1], (count, depth)), FLOOR)
            top = jnp.max(level, axis=1, keepdims=True)
            weight = jnp.where(match, jnp.exp(level - top), 0.0).astype(BF16)
            total = jnp.sum(weight.astype(F32), axis=1, keepdims=True)
            rows = ob[g][:, :, :, head_at(h)].astype(F32).reshape(depth, HD).astype(BF16)
            some = total > 0.0
            safe = jnp.where(some, total, 1.0)
            part = jnp.dot(weight, rows, preferred_element_type=F32) / safe
            cb[g][:, :, head_at(h)] = part.reshape(NZ, ROWS, HD).astype(BF16)
            tops = jnp.where(lane64 == h, jnp.where(some, top + jnp.log(safe), FLOOR), tops)
        cb[g][:, :, heads * HD :] = split3(tops).reshape(NZ, ROWS, 128).astype(BF16)
        b2.append(
            [
                go(
                    to_kv(
                        cb[g].at[z_at(d)], rb[g].at[z], b2_s.at[g * 8 + d], b2_r.at[g * 8 + d],
                        z_peer(d),
                    )
                )
                for d in FAR_FIRST
            ]
        )
        rb[g][z] = cb[g][z]

    b3 = []
    for g, (first, heads) in enumerate(GROUPS):
        arrive(*b2[g], self_copies[g])
        level = join3(rb[g][:, :, heads * HD :].astype(F32))
        share = jnp.exp(level - jnp.max(level, axis=0, keepdims=True))
        share = share / jnp.sum(share, axis=0, keepdims=True)
        for h in range(heads):
            part = share[:, :, h : h + 1] * rb[g][:, :, head_at(h)].astype(F32)
            az[g][z, :, head_at(h)] = jnp.sum(part, axis=0).astype(BF16)
        b3.append(
            [
                go(to_kv(az[g].at[z], az[g].at[z], b3_s.at[g * 8 + d], b3_r.at[g * 8 + d], z_peer(d)))
                for d in FAR_FIRST
            ]
        )
    late_on = weights_on(late, EARLY, chunks)
    large[0].wait()

    columns = chunks * 16

    def attended(g):
        arrive(*b3[g])
        return az[g][...].astype(F32).reshape(count, GROUPS[g][1] * HD).astype(BF16)

    def product(rows, e, g):
        block = wg[b_at(e)].reshape(columns, FEAT)[:, feats(g).start : feats(g).start + feats(g).size]
        return lax.dot_general(
            rows, block, (((1,), (1,)), ((), ())), preferred_element_type=F32
        )

    rows = attended(0)
    arrive(weight_own, *early_on, *late_on)
    for e in FAR_FIRST + (0,):
        acc[e, :, :columns] = product(rows, e, 0)
    rows = attended(1)
    c1 = []
    for e in FAR_FIRST + (0,):
        block = acc[e, :, :columns] + product(rows, e, 1)
        pc[e, :, :, :columns] = block.reshape(NZ, ROWS, columns).astype(BF16)
        for d in FAR_FIRST + (0,):
            band = lax.rem(t + d + 4, NT)
            if d == 0 and e == 0:
                fr[t * NB + b] = pc[e, band]
                continue
            pltpu.make_async_remote_copy(
                src_ref=pc.at[e, band], dst_ref=fr.at[t * NB + b], send_sem=c_s, recv_sem=c_r,
                device_id={"kv": b_peer(e), "tp": lax.rem(t + d, NT)}, device_id_type=MESH,
            ).start()
    for copy in sends:
        copy.wait_send()
    others = fr.at[pl.ds(0, NT * NB - 1)]
    every = to_kv(others, others, c_s, c_r, sibling)
    every.wait_recv()
    summed = jnp.sum(fr[...].astype(F32).reshape(NT, NB * ROWS, 128), axis=0)
    out_ref[:, :columns] = summed[:, :columns] + bias_ref[...].astype(F32).reshape(1, columns)
    every.wait_send()


def on_device(
    queries,
    new_keys,
    new_values,
    keys,
    values,
    slot_request,
    slot_valid,
    out_weight,
    out_bias,
    residual,
):
    slots = keys.shape[0]
    columns = out_weight.shape[1]
    pages = slots // PAGE
    blocks = pages // ROWS
    padded = 4
    vmem = pl.BlockSpec(memory_space=pltpu.VMEM)
    hbm = pl.BlockSpec(memory_space=pltpu.HBM)
    dma = pltpu.SemaphoreType.DMA

    def grouped(*lead, stats):
        return [
            pltpu.VMEM(lead + (heads * HD + (128 if stats else 0),), BF16) for _, heads in GROUPS
        ]

    projected = pl.pallas_call(
        kernel,
        out_shape=jax.ShapeDtypeStruct((NB * ROWS, 128), F32),
        in_specs=[hbm] * 9,
        out_specs=vmem,
        scratch_shapes=[
            pltpu.VMEM((columns,), BF16),
            pltpu.VMEM((ROWS, FEAT), BF16),
            pltpu.VMEM((ROWS, FEAT), BF16),
            pltpu.VMEM((slots,), jnp.int32),
            pltpu.VMEM((slots,), jnp.int32),
            pltpu.VMEM((slots, FEAT), BF16),
            pltpu.VMEM((slots, FEAT), BF16),
            pltpu.VMEM((NB, columns // 16, 16, FEAT), BF16),
            pltpu.VMEM((NX, pages, 128), F32),
            grouped(2, NZ, ROWS, stats=False),
            grouped(NX, blocks, ROWS, stats=False),
            grouped(NX, blocks, ROWS, stats=False),
            grouped(NB, padded, ROWS, stats=True),
            grouped(NZ, ROWS, stats=True),
            grouped(NZ + 1, ROWS, stats=True),
            grouped(ROWS, stats=True),
            grouped(NZ, ROWS, stats=False),
            pltpu.VMEM((NB, NZ * ROWS, 128), F32),
            pltpu.VMEM((NB, NZ, ROWS, 128), BF16),
            pltpu.VMEM((NT * NB, ROWS, 128), BF16),
            dma((10,)),
            dma((2 * NX,)), dma((2 * NX,)), dma((2 * NX,)), dma((2 * NX,)),
            dma((2,)), dma((2,)), dma((NX,)), dma((NX,)),
        ]
        + [dma((16,))] * 10
        + [dma((2,)), dma((2,)), dma, dma],
        compiler_params=pltpu.CompilerParams(
            collective_id=0, has_side_effects=True, vmem_limit_bytes=GRANT
        ),
        name="paged_decode",
    )(
        queries, new_keys, new_values, slot_request, slot_valid, keys, values,
        out_weight.T.reshape(columns // 16, 16, FEAT), out_bias,
    )
    total = residual.astype(F32) + projected[:, :columns]
    return total.astype(BF16)


def solution(mesh):
    placed = (
        P("kv", "tp"),
        P("kv", "tp"),
        P("kv", "tp"),
        P("kv", "tp"),
        P("kv", "tp"),
        P("kv"),
        P("kv"),
        P("tp", "kv"),
        P("kv"),
        P("tp", "kv"),
    )
    return jax.shard_map(
        on_device, mesh=mesh, in_specs=placed, out_specs=P("tp", "kv"), check_vma=False
    )
```

```python
import math

import jax
import jax.numpy as jnp
from jax import lax
from jax.experimental import pallas as pl
from jax.experimental.pallas import tpu as pltpu
from jax.sharding import PartitionSpec as P

HD = 128
HEADS = 7
FEAT = HEADS * HD
PAGE = 16
NX, NZ, NT, NB = 4, 8, 8, 8
ROWS = 8
FLOOR = -1e30
SCALE = 1.0 / math.sqrt(HD)
MESH = pl.DeviceIdType.MESH
F32, BF16 = jnp.float32, jnp.bfloat16

GROUPS = ((0, 2), (2, 5))

FAR_FIRST = (4, 3, 5, 2, 6, 1, 7)
X_FIRST = (2, 1, 3)

EARLY = 3

GRANT = 63 << 20


def kv_of(x, z, c):
    return (x * NZ + z) * 2 + c


def head_at(h):
    return slice(h * HD, (h + 1) * HD)


def split3(tile):
    lane = lax.broadcasted_iota(jnp.int32, tile.shape, 1)
    tile = jnp.where(lane < 8, tile, 0.0)
    high = tile.astype(BF16).astype(F32)
    middle = (tile - high).astype(BF16).astype(F32)
    low = tile - high - middle
    return high + pltpu.roll(middle, 8, 1) + pltpu.roll(low, 16, 1)


def join3(tile):
    axis = tile.ndim - 1
    return tile + pltpu.roll(tile, 128 - 8, axis) + pltpu.roll(tile, 128 - 16, axis)


def kernel(
    q_hbm, nk_hbm, nv_hbm, sr_hbm, sv_hbm, k_hbm, v_hbm, w_hbm, bias_hbm, out_ref,
    bias_ref, nk_ref, nv_ref, sr_ref, sv_ref, k_ref, v_ref, wg, idc, qz, qs, qr, ob, cb, rb, sb, az,
    acc, pc, fr, local, w_s, w_r, f_s, f_r, l_s, l_r, id_s, id_r, a1_s, a1_r, a2_s, a2_r, b1_s, b1_r,
    b2_s, b2_r, b3_s, b3_r, self_s, self_r, c_s, c_r,
):
    k = lax.axis_index("kv")
    t = lax.axis_index("tp")
    c = lax.rem(k, 2)
    xz = k // 2
    x = xz // NZ
    z = lax.rem(xz, NZ)
    b = x * 2 + c

    def to_kv(src, dst, send, recv, kv):
        return pltpu.make_async_remote_copy(
            src_ref=src, dst_ref=dst, send_sem=send, recv_sem=recv,
            device_id={"kv": kv}, device_id_type=MESH,
        )

    def z_at(d):
        return lax.rem(z + d, NZ)

    def b_at(e):
        return lax.rem(b + e, NB)

    def z_peer(d):
        return kv_of(x, z_at(d), c)

    def b_peer(e):
        other = b_at(e)
        return kv_of(other // 2, z, lax.rem(other, 2))

    def x_peer(d):
        return kv_of(lax.rem(x + d, NX), z, c)

    sibling = kv_of(x, z, 1 - c)
    owner = kv_of(lax.rem(z, 4), lax.rem(2 * x + z // 4 + 4, NZ), c)

    barrier = pltpu.get_barrier_semaphore()
    for d in FAR_FIRST:
        pl.semaphore_signal(barrier, inc=1, device_id={"kv": z_peer(d)}, device_id_type=MESH)
    for d in range(1, NX):
        pl.semaphore_signal(barrier, inc=1, device_id={"kv": x_peer(d)}, device_id_type=MESH)
    pl.semaphore_signal(barrier, inc=1, device_id={"kv": sibling}, device_id_type=MESH)
    for d in FAR_FIRST:
        pl.semaphore_signal(
            barrier, inc=1, device_id={"tp": lax.rem(t + d, NT)}, device_id_type=MESH
        )

    def feats(g):
        first, heads = GROUPS[g]
        return pl.ds(first * HD, heads * HD)

    groups = range(len(GROUPS))
    small = [
        pltpu.make_async_copy(sr_hbm, sr_ref, local.at[0]),
        pltpu.make_async_copy(sv_hbm, sv_ref, local.at[1]),
        pltpu.make_async_copy(nk_hbm, nk_ref, local.at[2]),
        pltpu.make_async_copy(nv_hbm, nv_ref, local.at[3]),
        pltpu.make_async_copy(bias_hbm, bias_ref, local.at[9]),
    ] + [
        pltpu.make_async_copy(q_hbm.at[:, feats(g)], qz[g].at[c, z], local.at[4 + g]) for g in groups
    ]
    large = [
        pltpu.make_async_copy(w_hbm, wg.at[b], local.at[6]),
        pltpu.make_async_copy(k_hbm, k_ref, local.at[7]),
        pltpu.make_async_copy(v_hbm, v_ref, local.at[8]),
    ]
    for load in small:
        load.start()

    sends = []

    def go(copy):
        copy.start()
        sends.append(copy)
        return copy

    def arrive(*copies):
        for copy in copies:
            copy.wait_recv()

    pl.semaphore_wait(barrier, 18)

    a1 = [
        [
            go(
                to_kv(
                    q_hbm.at[:, feats(g)], qz[g].at[c, z], a1_s.at[g * 8 + d], a1_r.at[g * 8 + d],
                    z_peer(d),
                )
            )
            for d in FAR_FIRST
        ]
        for g in groups
    ]

    slots = k_ref.shape[0]
    pages = slots // PAGE
    blocks = pages // ROWS
    lane_page = lax.broadcasted_iota(jnp.int32, (pages, slots), 1) // PAGE
    on_page = lane_page == lax.broadcasted_iota(jnp.int32, (pages, slots), 0)
    small[0].wait()
    request_row = jnp.broadcast_to(sr_ref[...].reshape(1, slots).astype(F32), (pages, slots))
    page_request = jnp.max(jnp.where(on_page, request_row, -1.0), axis=1, keepdims=True)
    idc[x] = jnp.broadcast_to(page_request, (pages, 128))
    ids = [go(to_kv(idc.at[x], idc.at[x], id_s.at[d], id_r.at[d], x_peer(d))) for d in X_FIRST]

    for load in large:
        load.start()

    def weights_x(first, last):
        part = pl.ds(first, last - first)
        sem = 0 if first == 0 else NX
        return [
            go(to_kv(w_hbm.at[part], wg.at[b, part], w_s.at[sem + d], w_r.at[sem + d], x_peer(d)))
            for d in X_FIRST
        ]

    def weights_on(copies, first, last):
        part = pl.ds(first, last - first)
        sem = 0 if first == 0 else NX
        done = []
        for copy, d in zip(copies, X_FIRST):
            arrive(copy)
            block = wg.at[lax.rem(x + NX - d, NX) * 2 + c, part]
            done.append(go(to_kv(block, block, f_s.at[sem + d], f_r.at[sem + d], sibling)))
        return done

    chunks = wg.shape[1]
    early = weights_x(0, EARLY)
    weight_own = go(to_kv(w_hbm, wg.at[b], w_s.at[0], w_r.at[0], sibling))

    for load in small[1:]:
        load.wait()
    live_row = jnp.broadcast_to(sv_ref[...].reshape(1, slots), (pages, slots))
    live = jnp.where(on_page, live_row, 0) == 1
    lane8 = lax.broadcasted_iota(jnp.int32, (ROWS, 128), 1)
    for g, (first, heads) in enumerate(GROUPS):
        own = jnp.zeros((ROWS, 128), F32)
        for h in range(heads):
            new_key = nk_ref[:, head_at(first + h)].astype(F32)
            product = qz[g][c, z, :, head_at(h)].astype(F32) * new_key
            own = jnp.where(lane8 == h, jnp.sum(product, axis=1, keepdims=True) * SCALE, own)
        sb[g][:, : heads * HD] = nv_ref[:, feats(g)]
        sb[g][:, heads * HD :] = split3(own).astype(BF16)
        ob[g][:, blocks:] = jnp.zeros((NB, ob[g].shape[1] - blocks) + ob[g].shape[2:], BF16)

    line_copies = []
    for g in groups:
        arrive(*a1[g])
        line = qz[g].at[c]
        line_copies.append(go(to_kv(line, line, l_s.at[g], l_r.at[g], sibling)))
    arrive(*ids)
    lane_q = lax.broadcasted_iota(jnp.int32, (NX * pages, 2 * NZ * ROWS), 1)
    core = lane_q // (NZ * ROWS)
    place = lax.rem(lane_q // ROWS, NZ) * 16 + core * ROWS + lax.rem(lane_q, ROWS)
    wanted = idc[...].reshape(NX * pages, 128)
    pick = jnp.where(wanted == (x * 128 + place).astype(F32), 1.0, 0.0).astype(BF16)
    a2 = []
    for g, (first, heads) in enumerate(GROUPS):
        arrive(line_copies[g])
        line = qz[g][...].astype(F32).reshape(2 * NZ * ROWS, heads * HD).astype(BF16)
        picked = jnp.dot(pick, line, preferred_element_type=F32)
        qs[g][...] = picked.reshape(NX, blocks, ROWS, heads * HD).astype(BF16)
        a2.append(
            [
                go(
                    to_kv(
                        qs[g].at[lax.rem(x + d, NX)], qr[g].at[x], a2_s.at[g * 8 + d],
                        a2_r.at[g * 8 + d], x_peer(d),
                    )
                )
                for d in X_FIRST
            ]
        )
        qr[g][x] = qs[g][x]

    large[1].wait()
    large[2].wait()
    lane24 = lax.broadcasted_iota(jnp.int32, (pages, 128), 1)
    b1, both = [], []
    for g, (first, heads) in enumerate(GROUPS):
        arrive(*a2[g])
        queries = jnp.sum(qr[g][...].astype(F32), axis=0).reshape(pages, heads * HD).astype(BF16)
        scores = [
            lax.dot_general(
                queries[:, head_at(h)], k_ref[:, head_at(first + h)], (((1,), (1,)), ((), ())),
                preferred_element_type=F32,
            )
            for h in range(heads)
        ]
        scores = [jnp.where(live, SCALE * score, FLOOR) for score in scores]
        top = [jnp.max(score, axis=1, keepdims=True) for score in scores]
        weights = [
            jnp.where(live, jnp.exp(score - high), 0.0).astype(BF16)
            for score, high in zip(scores, top)
        ]
        total = [jnp.sum(weight.astype(F32), axis=1, keepdims=True) for weight in weights]
        parts = [
            jnp.dot(weights[h], v_ref[:, head_at(first + h)], preferred_element_type=F32)
            for h in range(heads)
        ]
        tops = jnp.zeros((pages, 128), F32)
        for h in range(heads):
            part = (parts[h] / total[h]).reshape(blocks, ROWS, HD)
            ob[g][b, :blocks, :, head_at(h)] = part.astype(BF16)
            tops = jnp.where(lane24 == h, top[h] + jnp.log(total[h]), tops)
        stats = split3(tops)
        if g == 0:
            request_high = jnp.floor(page_request * 0.125)
            stats = jnp.where(lane24 == 24, request_high + 1.0, stats)
            stats = jnp.where(lane24 == 25, page_request - 8.0 * request_high, stats)
        stats = stats.reshape(blocks, ROWS, 128).astype(BF16)
        ob[g][b, :blocks, :, heads * HD :] = stats
        mine = ob[g].at[b, pl.ds(0, blocks)]
        b1.append(
            [
                go(to_kv(mine, mine, b1_s.at[g * 8 + d], b1_r.at[g * 8 + d], x_peer(d)))
                for d in X_FIRST
            ]
        )
        both.append([go(to_kv(mine, mine, b1_s.at[g * 8 + 4], b1_r.at[g * 8 + 4], sibling))])
    self_copies = [
        go(to_kv(sb[g], rb[g].at[NZ], self_s.at[g], self_r.at[g], owner)) for g in groups
    ]
    early_on = weights_on(early, 0, EARLY)

    for g in groups:
        for copy, d in zip(b1[g], X_FIRST):
            arrive(copy)
            block = ob[g].at[lax.rem(x + NX - d, NX) * 2 + c, pl.ds(0, blocks)]
            sem = g * 8 + 4 + d
            both[g].append(go(to_kv(block, block, b1_s.at[sem], b1_r.at[sem], sibling)))
    late = weights_x(EARLY, chunks)

    depth = NB * ob[0].shape[1] * ROWS
    count = NZ * ROWS
    lane64 = lax.broadcasted_iota(jnp.int32, (count, 128), 1)
    b2 = []
    for g, (first, heads) in enumerate(GROUPS):
        arrive(*both[g])
        turned = ob[g][:, :, :, heads * HD :].astype(F32).reshape(depth, 128).T
        row_top = turned[0:8] + turned[8:16] + turned[16:24]
        if g == 0:
            row_request = turned[24:25] * 8.0 + turned[25:26]
            row_q = lax.broadcasted_iota(jnp.int32, (count, depth), 0)
            my_request = (
                lax.rem(row_q // ROWS + 4, NZ) * 64 + b * ROWS + lax.rem(row_q, ROWS) + 8
            ).astype(F32)
            match = jnp.broadcast_to(row_request, (count, depth)) == my_request
        tops = jnp.full((count, 128), FLOOR, F32)
        for h in range(heads):
            level = jnp.where(match, jnp.broadcast_to(row_top[h : h + 1], (count, depth)), FLOOR)
            top = jnp.max(level, axis=1, keepdims=True)
            weight = jnp.where(match, jnp.exp(level - top), 0.0).astype(BF16)
            total = jnp.sum(weight.astype(F32), axis=1, keepdims=True)
            rows = ob[g][:, :, :, head_at(h)].astype(F32).reshape(depth, HD).astype(BF16)
            some = total > 0.0
            safe = jnp.where(some, total, 1.0)
            part = jnp.dot(weight, rows, preferred_element_type=F32) / safe
            cb[g][:, :, head_at(h)] = part.reshape(NZ, ROWS, HD).astype(BF16)
            tops = jnp.where(lane64 == h, jnp.where(some, top + jnp.log(safe), FLOOR), tops)
        cb[g][:, :, heads * HD :] = split3(tops).reshape(NZ, ROWS, 128).astype(BF16)
        b2.append(
            [
                go(
                    to_kv(
                        cb[g].at[z_at(d)], rb[g].at[z], b2_s.at[g * 8 + d], b2_r.at[g * 8 + d],
                        z_peer(d),
                    )
                )
                for d in FAR_FIRST
            ]
        )
        rb[g][z] = cb[g][z]

    b3 = []
    for g, (first, heads) in enumerate(GROUPS):
        arrive(*b2[g], self_copies[g])
        level = join3(rb[g][:, :, heads * HD :].astype(F32))
        share = jnp.exp(level - jnp.max(level, axis=0, keepdims=True))
        share = share / jnp.sum(share, axis=0, keepdims=True)
        for h in range(heads):
            part = share[:, :, h : h + 1] * rb[g][:, :, head_at(h)].astype(F32)
            az[g][z, :, head_at(h)] = jnp.sum(part, axis=0).astype(BF16)
        b3.append(
            [
                go(to_kv(az[g].at[z], az[g].at[z], b3_s.at[g * 8 + d], b3_r.at[g * 8 + d], z_peer(d)))
                for d in FAR_FIRST
            ]
        )
    late_on = weights_on(late, EARLY, chunks)
    large[0].wait()

    columns = chunks * 16

    def attended(g):
        arrive(*b3[g])
        return az[g][...].astype(F32).reshape(count, GROUPS[g][1] * HD).astype(BF16)

    def product(rows, e, g):
        block = wg[b_at(e)].reshape(columns, FEAT)[:, feats(g).start : feats(g).start + feats(g).size]
        return lax.dot_general(
            rows, block, (((1,), (1,)), ((), ())), preferred_element_type=F32
        )

    rows = attended(0)
    arrive(weight_own, *early_on, *late_on)
    for e in FAR_FIRST + (0,):
        acc[e, :, :columns] = product(rows, e, 0)
    rows = attended(1)
    c1 = []
    for e in FAR_FIRST + (0,):
        block = acc[e, :, :columns] + product(rows, e, 1)
        pc[e, :, :, :columns] = block.reshape(NZ, ROWS, columns).astype(BF16)
        for d in FAR_FIRST + (0,):
            band = lax.rem(t + d + 4, NT)
            if d == 0 and e == 0:
                fr[t * NB + b] = pc[e, band]
                continue
            pltpu.make_async_remote_copy(
                src_ref=pc.at[e, band], dst_ref=fr.at[t * NB + b], send_sem=c_s, recv_sem=c_r,
                device_id={"kv": b_peer(e), "tp": lax.rem(t + d, NT)}, device_id_type=MESH,
            ).start()
    for copy in sends:
        copy.wait_send()
    others = fr.at[pl.ds(0, NT * NB - 1)]
    every = to_kv(others, others, c_s, c_r, sibling)
    every.wait_recv()
    summed = jnp.sum(fr[...].astype(F32).reshape(NT, NB * ROWS, 128), axis=0)
    out_ref[:, :columns] = summed[:, :columns] + bias_ref[...].astype(F32).reshape(1, columns)
    every.wait_send()


def on_device(
    queries,
    new_keys,
    new_values,
    keys,
    values,
    slot_request,
    slot_valid,
    out_weight,
    out_bias,
    residual,
):
    slots = keys.shape[0]
    columns = out_weight.shape[1]
    pages = slots // PAGE
    blocks = pages // ROWS
    padded = 4
    vmem = pl.BlockSpec(memory_space=pltpu.VMEM)
    hbm = pl.BlockSpec(memory_space=pltpu.HBM)
    dma = pltpu.SemaphoreType.DMA

    def grouped(*lead, stats):
        return [
            pltpu.VMEM(lead + (heads * HD + (128 if stats else 0),), BF16) for _, heads in GROUPS
        ]

    projected = pl.pallas_call(
        kernel,
        out_shape=jax.ShapeDtypeStruct((NB * ROWS, 128), F32),
        in_specs=[hbm] * 9,
        out_specs=vmem,
        scratch_shapes=[
            pltpu.VMEM((columns,), BF16),
            pltpu.VMEM((ROWS, FEAT), BF16),
            pltpu.VMEM((ROWS, FEAT), BF16),
            pltpu.VMEM((slots,), jnp.int32),
            pltpu.VMEM((slots,), jnp.int32),
            pltpu.VMEM((slots, FEAT), BF16),
            pltpu.VMEM((slots, FEAT), BF16),
            pltpu.VMEM((NB, columns // 16, 16, FEAT), BF16),
            pltpu.VMEM((NX, pages, 128), F32),
            grouped(2, NZ, ROWS, stats=False),
            grouped(NX, blocks, ROWS, stats=False),
            grouped(NX, blocks, ROWS, stats=False),
            grouped(NB, padded, ROWS, stats=True),
            grouped(NZ, ROWS, stats=True),
            grouped(NZ + 1, ROWS, stats=True),
            grouped(ROWS, stats=True),
            grouped(NZ, ROWS, stats=False),
            pltpu.VMEM((NB, NZ * ROWS, 128), F32),
            pltpu.VMEM((NB, NZ, ROWS, 128), BF16),
            pltpu.VMEM((NT * NB, ROWS, 128), BF16),
            dma((10,)),
            dma((2 * NX,)), dma((2 * NX,)), dma((2 * NX,)), dma((2 * NX,)),
            dma((2,)), dma((2,)), dma((NX,)), dma((NX,)),
        ]
        + [dma((16,))] * 10
        + [dma((2,)), dma((2,)), dma, dma],
        compiler_params=pltpu.CompilerParams(
            collective_id=0, has_side_effects=True, vmem_limit_bytes=GRANT
        ),
        name="paged_decode",
    )(
        queries, new_keys, new_values, slot_request, slot_valid, keys, values,
        out_weight.T.reshape(columns // 16, 16, FEAT), out_bias,
    )
    total = residual.astype(F32) + projected[:, :columns]
    return total.astype(BF16)


def solution(mesh):
    placed = (
        P("kv", "tp"),
        P("kv", "tp"),
        P("kv", "tp"),
        P("kv", "tp"),
        P("kv", "tp"),
        P("kv"),
        P("kv"),
        P("tp", "kv"),
        P("kv"),
        P("tp", "kv"),
    )
    return jax.shard_map(
        on_device, mesh=mesh, in_specs=placed, out_specs=P("tp", "kv"), check_vma=False
    )
```
